1024 devices in a mesh: dom: 8 (over y_lo, core), band: 128 (over y_hi, z, x).
Axes of the slice: x: 4, y: 8 (y_hi: 2, y_lo: 4; y = y_hi * 4 + y_lo), z: 16, core: 2. Of those that a mesh axis runs over, the one named last changes fastest.
Arguments:
- psi_in: float32 [8, 128, 20, 1600], P('dom', 'band'), may hold values from -6 to 6
- v_in: float32 [8, 40, 1600], P('dom'), may hold values from -3 to 3
- offsets: int32 [8, 3], replicated, may hold values from 0 to 32, as said below
Outputs:
- psi_out: float32 [8, 128, 20, 1600], P('dom', 'band')
The draws below stay inside these ranges and needn't reach their ends.
Inputs may be any that keep to these rules, and one draw needn't show every extreme that they name: `offsets`: row d is the first corner of domain d's core in the global grid: its first two entries are 0 or 32, its third a multiple of 32 below 64; the 8 rows are distinct, so the cores tile the grid.
All inputs are finite; a program needn't handle non-finite values.
Results may differ from the reference program's by a relative error of at most 0.0003.
Values sent between devices are 32-bit elements; how exact they have to be, the bound alone decides.
A program may use at most 64 MiB of HBM per device.

```python
import math
import jax
import jax.numpy as jnp
from jax import lax

CORE = 32
BUF = 4
DEG = 8
NDOM = 8
BANDS = 64
SIDE = 40
SLAB = 20


def draw_offsets(key, part):
    order = jax.random.permutation(jax.random.fold_in(key, 17), jnp.arange(NDOM, dtype=jnp.int32))
    corner_x = order % 2 * CORE
    corner_y = order // 2 % 2 * CORE
    corner_z = order // 4 * CORE
    return jnp.stack([corner_x, corner_y, corner_z], 1).astype(jnp.int32)


def block_levels(stream_key, shape, split, smallest, top_value):
    def one(dim, blocks):
        heights = jax.random.uniform(jax.random.fold_in(jax.random.fold_in(stream_key, 6), dim), (blocks,), jnp.float32, smallest / len(split), top_value / len(split))
        return jnp.repeat(jnp.exp(heights), shape[dim] // blocks).reshape((-1,) + (1,) * (len(shape) - dim - 1))

    factor_of = one(*split[0])
    for cut in split[1:]:
        factor_of = factor_of * one(*cut)
    return factor_of


def normal_values(rng, extent, width, limit, split=(), kind=jnp.bfloat16):
    level = block_levels(rng, extent, split, -0.22, 0.18) if split else 1.0
    array = jax.random.normal(rng, extent, jnp.float32) * width * level
    return jnp.minimum(jnp.maximum(array, -limit), limit).astype(kind)


def setup_inputs(seed: int = 0) -> dict:
    keys = jax.random.split(jax.random.key(seed), 4)
    psi_in = normal_values(keys[0], (NDOM, 2 * BANDS, SLAB, SIDE * SIDE), 1.0, 6.0, ((0, 8), (1, 128)), jnp.float32)
    v_in = normal_values(keys[1], (NDOM, SIDE, SIDE * SIDE), 0.5, 3.0, ((0, 8),), jnp.float32)
    offsets = draw_offsets(jax.random.fold_in(keys[3], 71), 0)
    return dict(psi_in=psi_in, v_in=v_in, offsets=offsets)


CENTER = 3.0
HALF_WIDTH = 4.5
FOUR_PI = 4.0 * math.pi
EXCHANGE_COEF = -((3.0 / math.pi) ** (1.0 / 3.0))


def hamiltonian(values, potential):
    padded = jnp.pad(values, 1)
    beside_all = padded[2:, 1:-1, 1:-1] + padded[:-2, 1:-1, 1:-1]
    beside_all = beside_all + padded[1:-1, 2:, 1:-1] + padded[1:-1, :-2, 1:-1]
    beside_all = beside_all + padded[1:-1, 1:-1, 2:] + padded[1:-1, 1:-1, :-2]
    return 0.5 * (6.0 * values - beside_all) + potential * values


def shifted(values, potential):
    return (hamiltonian(values, potential) - CENTER * values) / HALF_WIDTH


def chebyshev(values, potential):
    previous = values
    current = shifted(values, potential)
    for order_idx in range(DEG - 1):
        following = 2.0 * shifted(current, potential) - previous
        previous, current = current, following
    return current


def reference(psi_in, v_in, offsets):
    side_len = CORE + 2 * BUF
    grid_x = 2 * CORE
    grid_z = CORE * NDOM // 4
    wavefunc = psi_in.reshape(NDOM, BANDS, side_len, side_len, side_len)
    potentials = v_in.reshape(NDOM, side_len, side_len, side_len)
    filter_all = jax.vmap(chebyshev, (0, None))

    def first_pass(domain_item):
        return filter_all(domain_item[0], domain_item[1])

    filtered = lax.map(first_pass, (wavefunc, potentials))
    cores = jnp.sum(filtered[:, :, BUF:BUF + CORE, BUF:BUF + CORE, BUF:BUF + CORE] ** 2, axis=1) / BANDS
    density = jnp.zeros((grid_x, grid_x, grid_z), jnp.float32)
    for dom_idx in range(NDOM):
        density = lax.dynamic_update_slice(density, cores[dom_idx], (offsets[dom_idx, 0], offsets[dom_idx, 1], offsets[dom_idx, 2]))
    spectrum = jnp.fft.fftn(density)
    modes_x = jnp.arange(grid_x)
    modes_z = jnp.arange(grid_z)
    eigen_x = 2.0 - 2.0 * jnp.cos(2.0 * math.pi * modes_x.astype(jnp.float32) / grid_x)
    eigen_z = 2.0 - 2.0 * jnp.cos(2.0 * math.pi * modes_z.astype(jnp.float32) / grid_z)
    eigen = eigen_x[:, None, None] + eigen_x[None, :, None] + eigen_z[None, None, :]
    zero_mode = (modes_x[:, None, None] == 0) & (modes_x[None, :, None] == 0) & (modes_z[None, None, :] == 0)
    factor = jnp.where(zero_mode, 0.0, FOUR_PI / jnp.where(zero_mode, 1.0, eigen))
    hartree = jnp.real(jnp.fft.ifftn(spectrum * factor)).astype(jnp.float32)

    def region(values, anchor):
        region_pos = jnp.arange(side_len, dtype=jnp.int32) - BUF
        index_x = ((anchor[0] + region_pos) % grid_x).astype(jnp.int32)
        index_y = ((anchor[1] + region_pos) % grid_x).astype(jnp.int32)
        index_z = ((anchor[2] + region_pos) % grid_z).astype(jnp.int32)
        return jnp.take(jnp.take(jnp.take(values, index_x, 0), index_y, 1), index_z, 2)

    def second_pass(domain_item):
        band_vals, potential, anchor = domain_item
        renewed = potential + region(hartree, anchor) + EXCHANGE_COEF * jnp.cbrt(region(density, anchor))
        return filter_all(band_vals, renewed)

    final = lax.map(second_pass, (filtered, potentials, offsets))
    return final.reshape(NDOM, 2 * BANDS, side_len // 2, side_len * side_len)
```

```python
import functools
import math

import jax
import jax.numpy as jnp
import numpy as np
from jax import lax
from jax.experimental import pallas as pl
from jax.experimental.pallas import tpu as pltpu
from jax.sharding import PartitionSpec as P

F32 = jnp.float32
MESH = pl.DeviceIdType.MESH
GRID = 64
SIDE = 40
BUF = 4
LANE = 128
GAP = 42
ROWS = 10
SLOTS = 28
HALO = 8
DEG = 8
HALF_WIDTH = 4.5
EXCHANGE = -((3.0 / math.pi) ** (1.0 / 3.0))
PART = 24


def wave_list():
    even = [("c", k) for k in range(0, 33, 2)] + [("s", k) for k in range(2, 32, 2)]
    odd = [("c", k) for k in range(1, 32, 2)] + [("s", k) for k in range(1, 32, 2)]
    return even + odd


def basis(cells):
    cells = np.asarray(cells, np.float64)
    rows = []
    for kind, k in wave_list():
        angle = 2.0 * np.pi * k * cells / GRID
        size = 1.0 if k in (0, 32) else 2.0
        rows.append(np.sqrt(size / GRID) * (np.cos(angle) if kind == "c" else np.sin(angle)))
    return np.stack(rows)


def tables():
    waves = np.array([k for _, k in wave_list()])
    lam = 2.0 - 2.0 * np.cos(2.0 * np.pi * waves / GRID)
    by = basis(np.arange(32))
    cz = np.tile(basis(np.arange(32)).T, (4, 2))
    cx = np.zeros((GRID, 4, 8, 2, 4))
    for q in range(4):
        for s in range(2):
            for t in range(4):
                n = 4 * t + q
                cx[:, q, :, s, t] = basis([n if s == 0 else 31 - n])
    cx = cx.reshape(GRID, 256)
    xall = np.zeros((3, 2, 2, ROWS, GRID))
    for g in range(3):
        for s in range(2):
            for r in range(ROWS):
                slot = ROWS * g + r
                if slot < SLOTS:
                    wave = basis([slot - BUF if s == 0 else 35 - slot])[:, 0]
                    xall[g, 0, s, r, :32] = wave[:32]
                    xall[g, 1, s, r, 32:] = wave[32:]
    xall = xall.reshape(120, GRID)
    zt = np.zeros((256, 2, LANE))
    region = basis(np.arange(SIDE) - BUF)
    for g in range(3):
        for b in range(2):
            zt[64 * g + 32 * b : 64 * g + 32 * b + 32, b, GAP * g : GAP * g + SIDE] = region[
                32 * b : 32 * b + 32
            ]
    zt = zt.reshape(256, 256)
    yt = region.T
    lam2 = np.concatenate(
        [lam[:32, None] + lam[None, :], lam[32:, None] + lam[None, :]], axis=1
    )
    out = (lam2, by, cz, cx, xall, zt, yt)
    return [np.asarray(a, np.float32) for a in out], np.asarray(lam, np.float32)


def lanes(shape):
    return lax.broadcasted_iota(jnp.int32, shape, len(shape) - 1)


def dot(a, b):
    return jnp.dot(a, b, precision=lax.Precision.HIGHEST, preferred_element_type=F32)


def roll(v, shift):
    shift %= LANE
    return v if shift == 0 else pltpu.roll(v, shift, 1)


def cbrt(x):
    a = jnp.abs(x)
    tiny = 1.2e-38
    b = jnp.maximum(a, tiny)
    y = jnp.exp(jnp.log(b) * (1.0 / 3.0))
    y = y - (y - b / (y * y)) * (1.0 / 3.0)
    y = jnp.where(a < tiny, 0.0, y)
    return jnp.where(x < 0.0, -y, y)


def line_of(ref, rows, y):
    block, at = divmod(SIDE * y, LANE)
    v = roll(ref[0:rows, block * LANE : (block + 1) * LANE], -at)
    if at + SIDE > LANE:
        w = roll(ref[0:rows, (block + 1) * LANE : (block + 2) * LANE], -at)
        v = jnp.where(lanes(v.shape) < LANE - at, v, w)
    return v


def to_tiles(ref, stride, row_of, tile):
    lane = lanes((SIDE, LANE))
    acc = jnp.zeros((SIDE, LANE), F32)
    for g in range(3):
        slot = ROWS * g + tile
        if slot < SLOTS:
            v = roll(ref[pl.ds(row_of(slot), SIDE, stride=stride), :], GAP * g)
            inside = (lane >= GAP * g) & (lane < GAP * g + SIDE)
            acc = jnp.where(inside, v, acc)
    return acc


def filter_step(src, dst, coef, first):
    lane = lanes((SIDE, LANE))
    inside = (lane < 3 * GAP) & (lane % GAP < SIDE)
    scale = (0.5 if first else 1.0) / HALF_WIDTH
    beta = jnp.where(inside, scale, 0.0).astype(F32)
    for r in range(ROWS):
        c = src[r, 8:48, :]
        if r == 0:
            below = jnp.where(lane >= GAP, roll(src[ROWS - 1, 8:48, :], GAP), 0.0)
        else:
            below = src[r - 1, 8:48, :]
        if r == ROWS - 1:
            above = roll(src[0, 8:48, :], -GAP)
        else:
            above = src[r + 1, 8:48, :]
        near = (below + above) + (src[r, 7:47, :] + src[r, 9:49, :])
        near = near + (roll(c, 1) + roll(c, -1))
        if first:
            dst[r, 8:48, :] = (0.5 * coef[r]) * c - beta * near
        else:
            dst[r, 8:48, :] = coef[r] * c - beta * near - dst[r, 8:48, :]


def chebyshev(buf_a, buf_b, coef):
    filter_step(buf_a, buf_b, coef, True)
    filter_step(buf_b, buf_a, coef, False)

    def two(_, carry):
        filter_step(buf_a, buf_b, coef, False)
        filter_step(buf_b, buf_a, coef, False)
        return carry

    lax.fori_loop(0, (DEG - 2) // 2, two, 0)


def clear_edges(buf):
    zero = jnp.zeros((8, LANE), F32)
    for r in range(ROWS):
        buf[r, 0:8, :] = zero
        buf[r, 48:56, :] = zero


def place():
    dom = lax.axis_index("dom")
    band = lax.axis_index("band")
    xi = lax.rem(band, 4)
    zi = lax.rem(band // 4, 16)
    yh = band // 64
    return dom, band, xi, zi, yh


def main_kernel(
    offs, lam_y, psi, pot, lam2, by, cz, cx, xall, zt, yt,
    field, coef_out,
    psi_pad, pot_pad, lines, pot_lines, h_send, h_recv, buf_a, buf_b, coef, squares,
    p_send, x_recv, y_send, y_recv, z_send, z_recv, z_all, r2_ref, c_send, c_recv, f_recv, h2_recv,
    h_sems, h2_sems, xs, xr, ys, yr, zs, zr, as_, ar, cs, cr, fs, fr,
):
    dom, band, xi, zi, yh = place()
    yc = yh * 8 + dom
    s = lax.rem(xi, 2)
    partner = xi + 1 - 2 * s

    def at_x(x):
        return (dom, band - xi + x)

    def at_z(z):
        return (dom, yh * 64 + z * 4 + xi)

    def at_y(c):
        return (lax.rem(c, 8), (c // 8) * 64 + zi * 4 + xi)

    def turn(value, n):
        return lax.rem(value + n, n)

    barrier = pltpu.get_barrier_semaphore()
    for o in range(1, 4):
        pl.semaphore_signal(barrier, inc=1, device_id=at_x(turn(xi + o, 4)), device_id_type=MESH)

    def greet(o, carry):
        pl.semaphore_signal(barrier, inc=1, device_id=at_z(turn(zi + o, 16)), device_id_type=MESH)
        pl.semaphore_signal(barrier, inc=1, device_id=at_y(turn(yc + o, 16)), device_id_type=MESH)
        return carry

    lax.fori_loop(1, 16, greet, 0)

    upper = s.astype(F32)
    h_send[:, 0:1600] = psi[12:20, :] * (1.0 - upper) + psi[0:8, :] * upper
    psi_pad[0:20, 0:1600] = psi[...]
    pot_pad[:, 0:1600] = pot[...]
    for y in range(SIDE):
        lines[y * 32 + 8 : y * 32 + 32, :] = line_of(psi_pad, 24, y)
    for y in range(SIDE):
        pot_lines[y * 40 : y * 40 + 40, :] = line_of(pot_pad, 40, y)
    clear_edges(buf_a)
    clear_edges(buf_b)
    for r in range(ROWS):
        coef[r] = to_tiles(
            pot_lines, 40, lambda slot: slot + s * (39 - 2 * slot), r
        ) * (2.0 / HALF_WIDTH)

    pl.semaphore_wait(barrier, 33)

    halo = pltpu.make_async_remote_copy(
        src_ref=h_send, dst_ref=h_recv, send_sem=h_sems.at[0], recv_sem=h_sems.at[1],
        device_id=at_x(partner), device_id_type=MESH,
    )
    halo.start()
    halo.wait()
    for y in range(SIDE):
        lines[y * 32 : y * 32 + 8, :] = line_of(h_recv, 8, y)

    def row_of(slot):
        if slot < 20:
            return 8 + slot + s * (19 - 2 * slot)
        return (slot - 20) + s * (47 - 2 * slot)

    for r in range(ROWS):
        buf_a[r, 8:48, :] = to_tiles(lines, 32, row_of, r)
    chebyshev(buf_a, buf_b, coef)

    lane32 = lanes((32, LANE))
    for t in range(4):
        acc = jnp.zeros((32, LANE), F32)
        for q in range(4):
            g, r = divmod(BUF + 4 * t + q, ROWS)
            v = roll(buf_a[r, 12:44, :], 32 * q - GAP * g - BUF)
            acc = jnp.where(lane32 // 32 == q, v, acc)
        squares[:, t * LANE : (t + 1) * LANE] = acc * acc * (1.0 / 64.0)

    def sign(d, axis):
        return 1.0 - offs[d, axis].astype(F32) * (1.0 / 16.0)

    sign_y = sign(dom, 1)
    odd_row = lax.broadcasted_iota(jnp.int32, (GRID, 32), 0) >= 32
    parts = dot(jnp.where(odd_row, sign_y, 1.0) * by[...], squares[...])
    for x in range(4):
        p_send[x] = parts[16 * x : 16 * x + 16]

    def x_copy(x, slot):
        return pltpu.make_async_remote_copy(
            src_ref=p_send.at[x], dst_ref=x_recv.at[slot], send_sem=xs.at[x],
            recv_sem=xr.at[slot], device_id=at_x(x), device_id_type=MESH,
        )

    for o in (2, 1, 3):
        x_copy(turn(xi + o, 4), xi).start()
    x_recv[xi] = p_send[xi]
    halo2 = pltpu.make_async_remote_copy(
        src_ref=buf_a.at[2:10, 8:48, :], dst_ref=h2_recv, send_sem=h2_sems.at[0],
        recv_sem=h2_sems.at[1], device_id=at_x(partner), device_id_type=MESH,
    )
    halo2.start()
    for o in (1, 3, 2):
        x_copy(turn(xi + o, 4), turn(xi - o + 4, 4)).wait_recv()
    for h in range(2):
        both = x_recv[h] + x_recv[h + 2]
        for t in range(4):
            y_send[pl.ds(h * 4 + t, 16, stride=8), :] = both[:, t * LANE : (t + 1) * LANE]

    def rows(index, size):
        return pl.ds(pl.multiple_of(index * size, 8), size)

    def y_copy(c, slot):
        return pltpu.make_async_remote_copy(
            src_ref=y_send.at[rows(c, 8)], dst_ref=y_recv.at[rows(slot, 8)], send_sem=ys.at[c],
            recv_sem=yr.at[slot], device_id=at_y(c), device_id_type=MESH,
        )

    def y_start(o, carry):
        y_copy(turn(yc + o, 16), yc).start()
        return carry

    def y_wait(o, carry):
        y_copy(turn(yc + o, 16), turn(yc - o + 16, 16)).wait_recv()
        return carry

    lax.fori_loop(1, 16, y_start, 0)
    y_recv[rows(yc, 8), :] = y_send[rows(yc, 8), :]
    lax.fori_loop(1, 16, y_wait, 0)

    d_all = y_recv[0:64, :] + y_recv[64:128, :]
    lane64 = lanes((64, LANE))
    masked = jnp.concatenate([jnp.where(lane64 // 32 == q, d_all, 0.0) for q in range(4)], 0)
    v_all = dot(masked, cz[...])
    lane8 = lanes((8, LANE))
    signs = []
    for d in range(8):
        sign_z = jnp.where(lane8 % 64 >= 32, sign(d, 2), 1.0)
        signs.append(sign_z * jnp.where(lane8 >= 64, sign(d, 0), 1.0))
    v_all = v_all * jnp.concatenate(signs * 4, 0)
    o_all = dot(cx[...], v_all)
    lane_r = lanes((32, LANE))
    left = lane_r < 64
    r2 = jnp.where(left, o_all[0:32], o_all[32:64])
    for k in range(16):
        z_send[k] = r2[2 * k : 2 * k + 2]

    def z_copy(z, slot):
        return pltpu.make_async_remote_copy(
            src_ref=z_send.at[z], dst_ref=z_recv.at[slot], send_sem=zs.at[z],
            recv_sem=zr.at[slot], device_id=at_z(z), device_id_type=MESH,
        )

    def z_start(o, carry):
        z_copy(turn(zi + o, 16), zi).start()
        return carry

    def z_wait(o, carry):
        z_copy(turn(zi + o, 16), turn(zi - o + 16, 16)).wait_recv()
        return carry

    lax.fori_loop(1, 16, z_start, 0)
    z_recv[zi] = z_send[zi]
    lax.fori_loop(1, 16, z_wait, 0)
    total = z_recv[0]
    for k in range(1, 16):
        total = total + z_recv[k]
    z_all[zi] = total

    def a_copy(z, slot):
        return pltpu.make_async_remote_copy(
            src_ref=z_all.at[zi], dst_ref=z_all.at[slot], send_sem=as_.at[z],
            recv_sem=ar.at[slot], device_id=at_z(z), device_id_type=MESH,
        )

    def a_start(o, carry):
        a_copy(turn(zi + o, 16), zi).start()
        return carry

    def a_wait(o, carry):
        a_copy(turn(zi + o, 16), turn(zi - o + 16, 16)).wait_recv()
        return carry

    lax.fori_loop(1, 16, a_start, 0)
    lax.fori_loop(1, 16, a_wait, 0)
    for k in range(16):
        r2_ref[2 * k : 2 * k + 2, :] = z_all[k]

    r2 = r2_ref[...]
    lam = lam2[...] + lam_y[xi * 16 + yc]
    factor = jnp.where(lam == 0.0, 0.0, 4.0 * math.pi / jnp.where(lam == 0.0, 1.0, lam))
    phi2 = r2 * factor
    top = jnp.where(left, r2, roll(phi2, 64))
    bottom = jnp.where(left, roll(r2, 64), phi2)
    t_all = dot(xall[...], jnp.concatenate([top, bottom], 0))
    t0, t1, t2 = t_all[0:40], t_all[40:80], t_all[80:120]
    left40 = lanes((40, LANE)) < 64
    of_rho = jnp.concatenate([jnp.where(left40, t0, roll(t1, 64)), t2], 1)
    of_phi = jnp.concatenate([jnp.where(left40, roll(t0, 64), t1), roll(t2, 64)], 1)
    planes = dot(jnp.concatenate([of_rho, of_phi], 0), zt[...])
    for d in range(8):
        both = planes[:, 0:LANE] + sign(d, 2) * planes[:, LANE : 2 * LANE]
        for f in range(2):
            rows20 = both[40 * f : 40 * f + 20] + sign(d, 0) * both[40 * f + 20 : 40 * f + 40]
            for h in range(2):
                at = (2 * d + h) * PART + 10 * f
                c_send[at : at + 10, :] = rows20[10 * h : 10 * h + 10]

    def c_copy(c, slot):
        return pltpu.make_async_remote_copy(
            src_ref=c_send.at[rows(lax.rem(c, 8), 2 * PART)],
            dst_ref=c_recv.at[rows(slot, 2 * PART)], send_sem=cs.at[c],
            recv_sem=cr.at[slot], device_id=at_y(c), device_id_type=MESH,
        )

    def c_start(o, carry):
        c_copy(turn(yc + o, 16), yc).start()
        return carry

    lax.fori_loop(1, 16, c_start, 0)
    c_recv[rows(yc, 2 * PART), :] = c_send[rows(dom, 2 * PART), :]

    def f_copy(x, c, from_x):
        return pltpu.make_async_remote_copy(
            src_ref=c_recv.at[rows(2 * c + lax.rem(x, 2), PART)],
            dst_ref=f_recv.at[rows(from_x * 16 + c, PART)],
            send_sem=fs.at[x * 16 + c], recv_sem=fr.at[from_x * 16 + c],
            device_id=at_x(x), device_id_type=MESH,
        )

    def forward(c):
        for o in (2, 1, 3):
            f_copy(turn(xi + o, 4), c, xi).start()
        f_recv[rows(xi * 16 + c, PART), :] = c_recv[rows(2 * c + s, PART), :]

    forward(yc)

    def c_wait(o, carry):
        c = turn(yc - o + 16, 16)
        c_copy(turn(yc + o, 16), c).wait_recv()
        forward(c)
        return carry

    lax.fori_loop(1, 16, c_wait, 0)

    halo2.wait()
    lane40 = lanes((SIDE, LANE))
    for r in range(ROWS):
        own = jnp.where(lane40 < 2 * GAP, buf_a[r, 8:48, :], 0.0)
        if r < HALO:
            inside = (lane40 >= 2 * GAP) & (lane40 < 2 * GAP + SIDE)
            own = jnp.where(inside, roll(h2_recv[HALO - 1 - r], GAP), own)
        field[r] = own

    def f_wait(c, carry):
        for o in (1, 3, 2):
            f_copy(turn(xi + o, 4), c, turn(xi - o + 4, 4)).wait_recv()
        return carry

    lax.fori_loop(0, 16, f_wait, 0)

    odd_col = lanes((SIDE, GRID)) >= 32
    to_y = jnp.where(odd_col, sign_y, 1.0) * yt[...]
    for r in range(ROWS):
        rho = dot(to_y, f_recv[pl.ds(r, GRID, stride=PART), :])
        phi = dot(to_y, f_recv[pl.ds(ROWS + r, GRID, stride=PART), :])
        coef_out[r] = coef[r] + (phi + EXCHANGE * cbrt(rho)) * (2.0 / HALF_WIDTH)

    for o in range(1, 4):
        x_copy(turn(xi + o, 4), xi).wait_send()

    def finish(o, carry):
        y_copy(turn(yc + o, 16), yc).wait_send()
        z_copy(turn(zi + o, 16), zi).wait_send()
        a_copy(turn(zi + o, 16), zi).wait_send()
        c_copy(turn(yc + o, 16), yc).wait_send()
        return carry

    lax.fori_loop(1, 16, finish, 0)

    def f_finish(c, carry):
        for o in range(1, 4):
            f_copy(turn(xi + o, 4), c, xi).wait_send()
        return carry

    lax.fori_loop(0, 16, f_finish, 0)


def last_kernel(field, coef, out, buf_a, buf_b, lines):
    band = lax.axis_index("band")
    s = lax.rem(band, 2)
    clear_edges(buf_a)
    clear_edges(buf_b)
    for r in range(ROWS):
        buf_a[r, 8:48, :] = field[r]
    chebyshev(buf_a, buf_b, coef)
    for slot in range(20):
        g, r = divmod(slot, ROWS)
        row = slot + s * (19 - 2 * slot)
        lines[pl.ds(row, SIDE, stride=24), :] = roll(buf_a[r, 8:48, :], -GAP * g)
    lane = lanes((24, LANE))
    for block in range(13):
        acc = jnp.zeros((24, LANE), F32)
        for y in range(SIDE):
            start = SIDE * y - LANE * block
            if start + SIDE > 0 and start < LANE:
                v = roll(lines[y * 24 : y * 24 + 24, :], start)
                inside = (lane >= start) & (lane < start + SIDE)
                acc = jnp.where(inside, v, acc)
        width = min(LANE, 1600 - LANE * block)
        out[:, block * LANE : block * LANE + width] = acc[0:20, 0:width]


def local(psi_in, v_in, offsets):
    consts, lam = tables()
    vmem = pl.BlockSpec(memory_space=pltpu.VMEM)
    smem = pl.BlockSpec(memory_space=pltpu.SMEM)
    dma = pltpu.SemaphoreType.DMA
    tile = jax.ShapeDtypeStruct((ROWS, SIDE, LANE), F32)

    def scratch(*shape):
        return pltpu.VMEM(shape, F32)

    field, coef = pl.pallas_call(
        main_kernel,
        out_shape=(tile, tile),
        in_specs=[smem, smem] + [vmem] * 9,
        out_specs=(vmem, vmem),
        scratch_shapes=[
            scratch(24, 1664), scratch(40, 1664), scratch(40 * 32, LANE), scratch(40 * 40, LANE),
            scratch(8, 1664), scratch(8, 1664), scratch(ROWS, 56, LANE), scratch(ROWS, 56, LANE),
            scratch(ROWS, SIDE, LANE), scratch(32, 512),
            scratch(4, 16, 512), scratch(4, 16, 512), scratch(128, LANE), scratch(128, LANE),
            scratch(16, 2, LANE), scratch(16, 2, LANE), scratch(16, 2, LANE), scratch(32, LANE),
            scratch(16 * PART, LANE), scratch(32 * PART, LANE), scratch(64 * PART, LANE),
            scratch(HALO, SIDE, LANE),
            dma((2,)), dma((2,)), dma((4,)), dma((4,)), dma((16,)), dma((16,)), dma((16,)),
            dma((16,)), dma((16,)), dma((16,)), dma((16,)), dma((16,)), dma((64,)), dma((64,)),
        ],
        compiler_params=pltpu.CompilerParams(collective_id=0, has_side_effects=True),
        name="step",
    )(offsets, jnp.asarray(lam), psi_in[0, 0], v_in[0], *[jnp.asarray(a) for a in consts])
    out = pl.pallas_call(
        last_kernel,
        out_shape=jax.ShapeDtypeStruct((20, 1600), F32),
        in_specs=[vmem, vmem],
        out_specs=vmem,
        scratch_shapes=[
            scratch(ROWS, 56, LANE), scratch(ROWS, 56, LANE), scratch(40 * 24, LANE),
        ],
        name="last",
    )(field, coef)
    return out[None, None]


def solution(mesh):
    return jax.shard_map(
        local,
        mesh=mesh,
        in_specs=(P("dom", "band", None, None), P("dom", None, None), P()),
        out_specs=P("dom", "band", None, None),
        check_vma=False,
    )
```

```python
import functools
import math

import jax
import jax.numpy as jnp
import numpy as np
from jax import lax
from jax.experimental import pallas as pl
from jax.experimental.pallas import tpu as pltpu
from jax.sharding import PartitionSpec as P

F32 = jnp.float32
MESH = pl.DeviceIdType.MESH
GRID = 64
SIDE = 40
BUF = 4
LANE = 128
GAP = 42
ROWS = 10
SLOTS = 28
HALO = 8
DEG = 8
HALF_WIDTH = 4.5
EXCHANGE = -((3.0 / math.pi) ** (1.0 / 3.0))
PART = 24
USED = 20
TABLES = 8
NEAR = [o for m in range(1, 8) for o in (m, 16 - m)] + [8]
FAR = NEAR[::-1]


def wave_list():
    even = [("c", k) for k in range(0, 33, 2)] + [("s", k) for k in range(2, 32, 2)]
    odd = [("c", k) for k in range(1, 32, 2)] + [("s", k) for k in range(1, 32, 2)]
    return even + odd


def basis(cells):
    cells = np.asarray(cells, np.float64)
    rows = []
    for kind, k in wave_list():
        angle = 2.0 * np.pi * k * cells / GRID
        size = 1.0 if k in (0, 32) else 2.0
        rows.append(np.sqrt(size / GRID) * (np.cos(angle) if kind == "c" else np.sin(angle)))
    return np.stack(rows)


def tables():
    waves = np.array([k for _, k in wave_list()])
    lam = 2.0 - 2.0 * np.cos(2.0 * np.pi * waves / GRID)
    by = basis(np.arange(32))
    cz = np.tile(basis(np.arange(32)).T, (4, 2))
    cx = np.zeros((GRID, 4, 8, 2, 4))
    for q in range(4):
        for s in range(2):
            for t in range(4):
                n = 4 * t + q
                cx[:, q, :, s, t] = basis([n if s == 0 else 31 - n])
    cx = cx.reshape(GRID, 256)
    xall = np.zeros((3, 2, 2, ROWS, GRID))
    for g in range(3):
        for s in range(2):
            for r in range(ROWS):
                slot = ROWS * g + r
                if slot < SLOTS:
                    wave = basis([slot - BUF if s == 0 else 35 - slot])[:, 0]
                    xall[g, 0, s, r, :32] = wave[:32]
                    xall[g, 1, s, r, 32:] = wave[32:]
    xall = xall.reshape(120, GRID)
    zt = np.zeros((256, 2, LANE))
    region = basis(np.arange(SIDE) - BUF)
    for g in range(3):
        for b in range(2):
            zt[64 * g + 32 * b : 64 * g + 32 * b + 32, b, GAP * g : GAP * g + SIDE] = region[
                32 * b : 32 * b + 32
            ]
    zt = zt.reshape(256, 256)
    yt = region.T
    lam2 = np.concatenate(
        [lam[:32, None] + lam[None, :], lam[32:, None] + lam[None, :]], axis=1
    )
    lam_y = np.repeat(lam[:, None], LANE, axis=1)
    out = (lam2, lam_y, by, cz, cx, xall, zt, yt)
    return [np.asarray(a, np.float32) for a in out]


def lanes(shape):
    return lax.broadcasted_iota(jnp.int32, shape, len(shape) - 1)


def dot(a, b):
    return jnp.dot(a, b, precision=lax.Precision.HIGHEST, preferred_element_type=F32)


def roll(v, shift):
    shift %= LANE
    return v if shift == 0 else pltpu.roll(v, shift, 1)


def cbrt(x):
    a = jnp.abs(x)
    tiny = 1.2e-38
    b = jnp.maximum(a, tiny)
    y = jnp.exp(jnp.log(b) * (1.0 / 3.0))
    y = y - (y - b / (y * y)) * (1.0 / 3.0)
    y = jnp.where(a < tiny, 0.0, y)
    return jnp.where(x < 0.0, -y, y)


def line_of(ref, rows, y):
    block, at = divmod(SIDE * y, LANE)
    v = roll(ref[0:rows, block * LANE : (block + 1) * LANE], -at)
    if at + SIDE > LANE:
        w = roll(ref[0:rows, (block + 1) * LANE : (block + 2) * LANE], -at)
        v = jnp.where(lanes(v.shape) < LANE - at, v, w)
    return v


def to_tiles(ref, stride, row_of, tile):
    lane = lanes((SIDE, LANE))
    acc = jnp.zeros((SIDE, LANE), F32)
    for g in range(3):
        slot = ROWS * g + tile
        if slot < SLOTS:
            v = roll(ref[pl.ds(row_of(slot), SIDE, stride=stride), :], GAP * g)
            inside = (lane >= GAP * g) & (lane < GAP * g + SIDE)
            acc = jnp.where(inside, v, acc)
    return acc


def filter_step(src, dst, coef, first):
    lane = lanes((SIDE, LANE))
    inside = (lane < 3 * GAP) & (lane % GAP < SIDE)
    scale = (0.5 if first else 1.0) / HALF_WIDTH
    beta = jnp.where(inside, scale, 0.0).astype(F32)
    for r in range(ROWS):
        c = src[r, 8:48, :]
        if r == 0:
            below = jnp.where(lane >= GAP, roll(src[ROWS - 1, 8:48, :], GAP), 0.0)
        else:
            below = src[r - 1, 8:48, :]
        if r == ROWS - 1:
            above = roll(src[0, 8:48, :], -GAP)
        else:
            above = src[r + 1, 8:48, :]
        near = (below + above) + (src[r, 7:47, :] + src[r, 9:49, :])
        near = near + (roll(c, 1) + roll(c, -1))
        if first:
            dst[r, 8:48, :] = (0.5 * coef[r]) * c - beta * near
        else:
            dst[r, 8:48, :] = coef[r] * c - beta * near - dst[r, 8:48, :]


def chebyshev(buf_a, buf_b, coef):
    filter_step(buf_a, buf_b, coef, True)
    filter_step(buf_b, buf_a, coef, False)

    def two(_, carry):
        filter_step(buf_a, buf_b, coef, False)
        filter_step(buf_b, buf_a, coef, False)
        return carry

    lax.fori_loop(0, (DEG - 2) // 2, two, 0)


def clear_edges(buf):
    zero = jnp.zeros((8, LANE), F32)
    for r in range(ROWS):
        buf[r, 0:8, :] = zero
        buf[r, 48:56, :] = zero


def place():
    dom = lax.axis_index("dom")
    band = lax.axis_index("band")
    xi = lax.rem(band, 4)
    zi = lax.rem(band // 4, 16)
    yh = band // 64
    return dom, band, xi, zi, yh


def main_kernel(
    offs_in, psi, pot, *rest
):
    sources, rest = rest[:TABLES], rest[TABLES:]
    field, coef_out, *rest = rest
    copies, rest = rest[:TABLES], rest[TABLES:]
    lam2, lam_y, by, cz, cx, xall, zt, yt = copies
    (
    offs, psi_raw, pot_raw, in_sems, psi_pad, pot_pad, lines, pot_lines, h_send, h_recv, buf_a, buf_b, coef, squares,
    p_send, x_recv, y_send, y_recv, z_send, z_recv, z_all, r2_ref, c_send, c_recv, f_recv, h2_recv,
    h_sems, h2_sems, xs, xr, ys, yr, zs, zr, as_, ar, cs, cr, fs, fr,
    ) = rest
    loads = [
        pltpu.make_async_copy(a, b, in_sems.at[n])
        for n, (a, b) in enumerate(zip((psi, pot, offs_in, *sources), (psi_raw, pot_raw, offs, *copies)))
    ]
    dom, band, xi, zi, yh = place()
    yc = yh * 8 + dom
    s = lax.rem(xi, 2)
    partner = xi + 1 - 2 * s

    def at_x(x):
        return (dom, band - xi + x)

    def at_z(z):
        return (dom, yh * 64 + z * 4 + xi)

    def at_y(c):
        high = jnp.where(c >= 8, 1, 0)
        return (c - 8 * high, high * 64 + zi * 4 + xi)

    def turn(value, n):
        return jnp.where(value >= n, value - n, value)

    barrier = pltpu.get_barrier_semaphore()
    for o in FAR:
        to = at_z(turn(zi + o, 16))
        pl.semaphore_signal(barrier, inc=1, device_id=to, device_id_type=MESH)
    for o in FAR:
        to = at_y(turn(yc + o, 16))
        pl.semaphore_signal(barrier, inc=1, device_id=to, device_id_type=MESH)
    for o in (2, 1, 3):
        pl.semaphore_signal(barrier, inc=1, device_id=at_x(turn(xi + o, 4)), device_id_type=MESH)
    for load in loads:
        load.start()

    upper = s.astype(F32)
    loads[0].wait()
    psi_pad[0:20, 0:1600] = psi_raw[...].reshape(20, 1600)
    h_send[...] = psi_pad[12:20, :] * (1.0 - upper) + psi_pad[0:8, :] * upper
    loads[1].wait()
    pot_pad[:, 0:1600] = pot_raw[...]
    for y in range(SIDE):
        lines[y * 32 + 8 : y * 32 + 32, :] = line_of(psi_pad, 24, y)
    for y in range(SIDE):
        pot_lines[y * 40 : y * 40 + 40, :] = line_of(pot_pad, 40, y)
    clear_edges(buf_a)
    clear_edges(buf_b)
    for r in range(ROWS):
        coef[r] = to_tiles(
            pot_lines, 40, lambda slot: slot + s * (39 - 2 * slot), r
        ) * (2.0 / HALF_WIDTH)

    for load in loads[2:]:
        load.wait()
    pl.semaphore_wait(barrier, 33)

    halo = pltpu.make_async_remote_copy(
        src_ref=h_send, dst_ref=h_recv, send_sem=h_sems.at[0], recv_sem=h_sems.at[1],
        device_id=at_x(partner), device_id_type=MESH,
    )
    halo.start()
    halo.wait()
    for y in range(SIDE):
        lines[y * 32 : y * 32 + 8, :] = line_of(h_recv, 8, y)

    def row_of(slot):
        if slot < 20:
            return 8 + slot + s * (19 - 2 * slot)
        return (slot - 20) + s * (47 - 2 * slot)

    for r in range(ROWS):
        buf_a[r, 8:48, :] = to_tiles(lines, 32, row_of, r)
    chebyshev(buf_a, buf_b, coef)

    lane32 = lanes((32, LANE))
    for t in range(4):
        acc = jnp.zeros((32, LANE), F32)
        for q in range(4):
            g, r = divmod(BUF + 4 * t + q, ROWS)
            v = roll(buf_a[r, 12:44, :], 32 * q - GAP * g - BUF)
            acc = jnp.where(lane32 // 32 == q, v, acc)
        squares[:, t * LANE : (t + 1) * LANE] = acc * acc * (1.0 / 64.0)

    corners = 1.0 - offs[...].astype(F32) * (1.0 / 16.0)

    def sign(d, axis):
        return corners[axis : axis + 1, d : d + 1]

    own_dom = lax.broadcasted_iota(jnp.int32, (1, 8), 1) == dom
    sign_y = jnp.sum(jnp.where(own_dom, corners[1:2], 0.0), axis=1, keepdims=True)
    odd_row = lax.broadcasted_iota(jnp.int32, (GRID, 32), 0) >= 32
    parts = dot(jnp.where(odd_row, sign_y, 1.0) * by[...], squares[...])
    for x in range(4):
        p_send[x] = parts[16 * x : 16 * x + 16]

    def x_copy(x, slot):
        return pltpu.make_async_remote_copy(
            src_ref=p_send.at[x], dst_ref=x_recv.at[slot], send_sem=xs.at[x],
            recv_sem=xr.at[slot], device_id=at_x(x), device_id_type=MESH,
        )

    for o in (2, 1, 3):
        x_copy(turn(xi + o, 4), xi).start()
    x_recv[xi] = p_send[xi]
    halo2 = pltpu.make_async_remote_copy(
        src_ref=buf_a.at[2:10, 8:48, :], dst_ref=h2_recv, send_sem=h2_sems.at[0],
        recv_sem=h2_sems.at[1], device_id=at_x(partner), device_id_type=MESH,
    )
    halo2.start()
    for o in (1, 3, 2):
        x_copy(turn(xi + o, 4), turn(xi - o + 4, 4)).wait_recv()
    for h in range(2):
        both = x_recv[h] + x_recv[h + 2]
        for t in range(4):
            y_send[pl.ds(h * 4 + t, 16, stride=8), :] = both[:, t * LANE : (t + 1) * LANE]

    def rows(index, size):
        return pl.ds(pl.multiple_of(index * size, 8), size)

    def y_copy(c, slot):
        return pltpu.make_async_remote_copy(
            src_ref=y_send.at[rows(c, 8)], dst_ref=y_recv.at[rows(slot, 8)], send_sem=ys,
            recv_sem=yr, device_id=at_y(c), device_id_type=MESH,
        )

    def whole(ref, send_sem, recv_sem):
        return pltpu.make_async_remote_copy(
            src_ref=ref, dst_ref=ref, send_sem=send_sem, recv_sem=recv_sem,
            device_id=at_x(partner), device_id_type=MESH,
        )

    y_whole = whole(y_recv.at[0:120], ys, yr)
    z_whole = whole(z_recv.at[0:15], zs, zr)
    a_whole = whole(z_all.at[0:15], as_, ar)
    f_whole = whole(f_recv.at[0 : 48 * USED], fs, fr)

    for o in FAR:
        y_copy(turn(yc + o, 16), yc).start()
    y_recv[rows(yc, 8), :] = y_send[rows(yc, 8), :]
    y_whole.wait_recv()

    d_all = y_recv[0:64, :] + y_recv[64:128, :]
    lane64 = lanes((64, LANE))
    masked = jnp.concatenate([jnp.where(lane64 // 32 == q, d_all, 0.0) for q in range(4)], 0)
    v_all = dot(masked, cz[...])
    lane8 = lanes((8, LANE))
    signs = []
    for d in range(8):
        sign_z = jnp.where(lane8 % 64 >= 32, sign(d, 2), 1.0)
        signs.append(sign_z * jnp.where(lane8 >= 64, sign(d, 0), 1.0))
    v_all = v_all * jnp.concatenate(signs * 4, 0)
    o_all = dot(cx[...], v_all)
    lane_r = lanes((32, LANE))
    left = lane_r < 64
    r2 = jnp.where(left, o_all[0:32], o_all[32:64])
    for k in range(16):
        z_send[k] = r2[2 * k : 2 * k + 2]

    def z_copy(z, slot):
        return pltpu.make_async_remote_copy(
            src_ref=z_send.at[z], dst_ref=z_recv.at[slot], send_sem=zs,
            recv_sem=zr, device_id=at_z(z), device_id_type=MESH,
        )

    for o in FAR:
        z_copy(turn(zi + o, 16), zi).start()
    z_recv[zi] = z_send[zi]
    z_whole.wait_recv()
    total = z_recv[0]
    for k in range(1, 16):
        total = total + z_recv[k]
    z_all[zi] = total

    def a_copy(z, slot):
        return pltpu.make_async_remote_copy(
            src_ref=z_all.at[zi], dst_ref=z_all.at[slot], send_sem=as_,
            recv_sem=ar, device_id=at_z(z), device_id_type=MESH,
        )

    for o in FAR:
        a_copy(turn(zi + o, 16), zi).start()
    a_whole.wait_recv()
    for k in range(16):
        r2_ref[2 * k : 2 * k + 2, :] = z_all[k]

    r2 = r2_ref[...]
    lam = lam2[...] + lam_y[pl.ds(xi * 16 + yc, 1), :]
    factor = jnp.where(lam == 0.0, 0.0, 4.0 * math.pi / jnp.where(lam == 0.0, 1.0, lam))
    phi2 = r2 * factor
    top = jnp.where(left, r2, roll(phi2, 64))
    bottom = jnp.where(left, roll(r2, 64), phi2)
    t_all = dot(xall[...], jnp.concatenate([top, bottom], 0))
    t0, t1, t2 = t_all[0:40], t_all[40:80], t_all[80:120]
    left40 = lanes((40, LANE)) < 64
    of_rho = jnp.concatenate([jnp.where(left40, t0, roll(t1, 64)), t2], 1)
    of_phi = jnp.concatenate([jnp.where(left40, roll(t0, 64), t1), roll(t2, 64)], 1)
    planes = dot(jnp.concatenate([of_rho, of_phi], 0), zt[...])
    for d in range(8):
        both = planes[:, 0:LANE] + sign(d, 2) * planes[:, LANE : 2 * LANE]
        for f in range(2):
            rows20 = both[40 * f : 40 * f + 20] + sign(d, 0) * both[40 * f + 20 : 40 * f + 40]
            for h in range(2):
                at = (2 * d + h) * PART + 10 * f
                c_send[at : at + 10, :] = rows20[10 * h : 10 * h + 10]

    def used(index):
        return pl.ds(pl.multiple_of(index * PART, 8), USED)

    def c_copy(c, slot, h):
        return pltpu.make_async_remote_copy(
            src_ref=c_send.at[used(2 * (c - jnp.where(c >= 8, 8, 0)) + h)],
            dst_ref=c_recv.at[used(2 * slot + h)], send_sem=cs,
            recv_sem=cr.at[slot], device_id=at_y(c), device_id_type=MESH,
        )

    for o in NEAR:
        for h in range(2):
            c_copy(turn(yc + o, 16), yc, h).start()
    c_recv[rows(yc, 2 * PART), :] = c_send[rows(dom, 2 * PART), :]

    def f_copy(x, h, c, from_x):
        return pltpu.make_async_remote_copy(
            src_ref=c_recv.at[used(2 * c + h)],
            dst_ref=f_recv.at[used(from_x * 16 + c)],
            send_sem=fs, recv_sem=fr,
            device_id=at_x(x), device_id_type=MESH,
        )

    def forward(c):
        for o in (2, 1, 3):
            f_copy(turn(xi + o, 4), s if o == 2 else 1 - s, c, xi).start()
        f_recv[rows(xi * 16 + c, PART), :] = c_recv[rows(2 * c + s, PART), :]

    forward(yc)

    y_whole.wait_send()
    z_whole.wait_send()
    a_whole.wait_send()
    for o in range(1, 4):
        x_copy(turn(xi + o, 4), xi).wait_send()

    for o in NEAR:
        c = turn(yc - o + 16, 16)
        whole(c_recv.at[0 : 2 * USED], cs, cr.at[c]).wait_recv()
        forward(c)

    halo2.wait()
    lane40 = lanes((SIDE, LANE))
    for r in range(ROWS):
        own = jnp.where(lane40 < 2 * GAP, buf_a[r, 8:48, :], 0.0)
        if r < HALO:
            inside = (lane40 >= 2 * GAP) & (lane40 < 2 * GAP + SIDE)
            own = jnp.where(inside, roll(h2_recv[HALO - 1 - r], GAP), own)
        field[r] = own

    f_whole.wait_recv()

    odd_col = lanes((SIDE, GRID)) >= 32
    to_y = jnp.where(odd_col, sign_y, 1.0) * yt[...]
    for r in range(ROWS):
        rho = dot(to_y, f_recv[pl.ds(r, GRID, stride=PART), :])
        phi = dot(to_y, f_recv[pl.ds(ROWS + r, GRID, stride=PART), :])
        coef_out[r] = coef[r] + (phi + EXCHANGE * cbrt(rho)) * (2.0 / HALF_WIDTH)
    whole(c_recv.at[0 : 30 * USED], cs, cs).wait_send()
    f_whole.wait_send()


def last_kernel(field, coef, out, buf_a, buf_b, lines):
    band = lax.axis_index("band")
    s = lax.rem(band, 2)
    clear_edges(buf_a)
    clear_edges(buf_b)
    for r in range(ROWS):
        buf_a[r, 8:48, :] = field[r]
    chebyshev(buf_a, buf_b, coef)
    for slot in range(20):
        g, r = divmod(slot, ROWS)
        row = slot + s * (19 - 2 * slot)
        lines[pl.ds(row, SIDE, stride=24), :] = roll(buf_a[r, 8:48, :], -GAP * g)
    lane = lanes((24, LANE))
    for block in range(13):
        acc = jnp.zeros((24, LANE), F32)
        for y in range(SIDE):
            start = SIDE * y - LANE * block
            if start + SIDE > 0 and start < LANE:
                v = roll(lines[y * 24 : y * 24 + 24, :], start)
                inside = (lane >= start) & (lane < start + SIDE)
                acc = jnp.where(inside, v, acc)
        width = min(LANE, 1600 - LANE * block)
        for x in range(20):
            out[x, :, block * LANE : block * LANE + width] = acc[x : x + 1, 0:width]


def local(psi_in, v_in, offsets):
    consts = tables()
    vmem = pl.BlockSpec(memory_space=pltpu.VMEM)
    dma = pltpu.SemaphoreType.DMA
    tile = jax.ShapeDtypeStruct((ROWS, SIDE, LANE), F32)

    def scratch(*shape):
        return pltpu.VMEM(shape, F32)

    operands = (
        offsets.T, jnp.swapaxes(psi_in[0], 0, 1), v_in[0], *[jnp.asarray(a) for a in consts]
    )
    field, coef = pl.pallas_call(
        main_kernel,
        out_shape=(tile, tile),
        in_specs=[pl.BlockSpec(memory_space=pltpu.HBM)] * (3 + TABLES),
        out_specs=(vmem, vmem),
        scratch_shapes=[
            *[scratch(*a.shape) for a in consts], pltpu.VMEM((3, 8), jnp.int32),
            scratch(20, 1, 1600), scratch(40, 1600), dma((3 + TABLES,)),
            scratch(24, 1664), scratch(40, 1664), scratch(40 * 32, LANE), scratch(40 * 40, LANE),
            scratch(8, 1664), scratch(8, 1664), scratch(ROWS, 56, LANE), scratch(ROWS, 56, LANE),
            scratch(ROWS, SIDE, LANE), scratch(32, 512),
            scratch(4, 16, 512), scratch(4, 16, 512), scratch(128, LANE), scratch(128, LANE),
            scratch(16, 2, LANE), scratch(16, 2, LANE), scratch(16, 2, LANE), scratch(32, LANE),
            scratch(16 * PART, LANE), scratch(32 * PART, LANE), scratch(64 * PART, LANE),
            scratch(HALO, SIDE, LANE),
            dma((2,)), dma((2,)), dma((4,)), dma((4,)), dma, dma, dma, dma, dma, dma,
            dma, dma((16,)), dma, dma,
        ],
        compiler_params=pltpu.CompilerParams(collective_id=0, has_side_effects=True, vmem_limit_bytes=24 << 20
        ),
        name="step",
    )(*[pltpu.with_memory_space_constraint(a, pltpu.HBM) for a in operands])
    out = pl.pallas_call(
        last_kernel,
        out_shape=jax.ShapeDtypeStruct((20, 1, 1600), F32),
        in_specs=[vmem, vmem],
        out_specs=vmem,
        scratch_shapes=[
            scratch(ROWS, 56, LANE), scratch(ROWS, 56, LANE), scratch(40 * 24, LANE),
        ],
        compiler_params=pltpu.CompilerParams(vmem_limit_bytes=8 << 20),
        name="last",
    )(field, coef)
    return jnp.swapaxes(out, 0, 1)[None]


def solution(mesh):
    return jax.shard_map(
        local,
        mesh=mesh,
        in_specs=(P("dom", "band", None, None), P("dom", None, None), P()),
        out_specs=P("dom", "band", None, None),
        check_vma=False,
    )
```

```python
import functools
import math

import jax
import jax.numpy as jnp
import numpy as np
from jax import lax
from jax.experimental import pallas as pl
from jax.experimental.pallas import tpu as pltpu
from jax.sharding import PartitionSpec as P

F32 = jnp.float32
MESH = pl.DeviceIdType.MESH
GRID = 64
SIDE = 40
BUF = 4
LANE = 128
GAP = 42
ROWS = 10
SLOTS = 28
HALO = 8
DEG = 8
HALF_WIDTH = 4.5
EXCHANGE = -((3.0 / math.pi) ** (1.0 / 3.0))
PART = 24
USED = 20
TABLES = 8
NEAR = [o for m in range(1, 8) for o in (m, 16 - m)] + [8]
FAR = NEAR[::-1]
FIRST_SUM = 12
SUM_TO = (0, 1, 2, 3, 4, 11, 5, 10, 6, 9, 7, 8, 12, 13, 14, 15)


def wave_list():
    even = [("c", k) for k in range(0, 33, 2)] + [("s", k) for k in range(2, 32, 2)]
    odd = [("c", k) for k in range(1, 32, 2)] + [("s", k) for k in range(1, 32, 2)]
    return even + odd


def basis(cells):
    cells = np.asarray(cells, np.float64)
    rows = []
    for kind, k in wave_list():
        angle = 2.0 * np.pi * k * cells / GRID
        size = 1.0 if k in (0, 32) else 2.0
        rows.append(np.sqrt(size / GRID) * (np.cos(angle) if kind == "c" else np.sin(angle)))
    return np.stack(rows)


def tables():
    waves = np.array([k for _, k in wave_list()])
    lam = 2.0 - 2.0 * np.cos(2.0 * np.pi * waves / GRID)
    by = basis(np.arange(32))
    cz = np.tile(basis(np.arange(32)).T, (4, 2))
    cx = np.zeros((GRID, 4, 8, 2, 4))
    for q in range(4):
        for s in range(2):
            for t in range(4):
                n = 4 * t + q
                cx[:, q, :, s, t] = basis([n if s == 0 else 31 - n])
    cx = cx.reshape(GRID, 256)
    xall = np.zeros((3, 2, 2, ROWS, GRID))
    for g in range(3):
        for s in range(2):
            for r in range(ROWS):
                slot = ROWS * g + r
                if slot < SLOTS:
                    wave = basis([slot - BUF if s == 0 else 35 - slot])[:, 0]
                    xall[g, 0, s, r, :32] = wave[:32]
                    xall[g, 1, s, r, 32:] = wave[32:]
    xall = xall.reshape(120, GRID)
    zt = np.zeros((256, 2, LANE))
    region = basis(np.arange(SIDE) - BUF)
    for g in range(3):
        for b in range(2):
            zt[64 * g + 32 * b : 64 * g + 32 * b + 32, b, GAP * g : GAP * g + SIDE] = region[
                32 * b : 32 * b + 32
            ]
    zt = zt.reshape(256, 256)
    yt = region.T
    lam2 = np.concatenate(
        [lam[:32, None] + lam[None, :], lam[32:, None] + lam[None, :]], axis=1
    )
    lam_y = np.repeat(lam[:, None], LANE, axis=1)
    out = (lam2, lam_y, by, cz, cx, xall, zt, yt)
    return [np.asarray(a, np.float32) for a in out]


def lanes(shape):
    return lax.broadcasted_iota(jnp.int32, shape, len(shape) - 1)


def dot(a, b):
    return jnp.dot(a, b, precision=lax.Precision.HIGHEST, preferred_element_type=F32)


def roll(v, shift):
    shift %= LANE
    return v if shift == 0 else pltpu.roll(v, shift, 1)


def cbrt(x):
    a = jnp.abs(x)
    tiny = 1.2e-38
    b = jnp.maximum(a, tiny)
    y = jnp.exp(jnp.log(b) * (1.0 / 3.0))
    y = y - (y - b / (y * y)) * (1.0 / 3.0)
    y = jnp.where(a < tiny, 0.0, y)
    return jnp.where(x < 0.0, -y, y)


def line_of(ref, rows, y):
    block, at = divmod(SIDE * y, LANE)
    v = roll(ref[0:rows, block * LANE : (block + 1) * LANE], -at)
    if at + SIDE > LANE:
        w = roll(ref[0:rows, (block + 1) * LANE : (block + 2) * LANE], -at)
        v = jnp.where(lanes(v.shape) < LANE - at, v, w)
    return v


def to_tiles(ref, stride, row_of, tile, groups=(0, 1, 2), acc=None):
    lane = lanes((SIDE, LANE))
    if acc is None:
        acc = jnp.zeros((SIDE, LANE), F32)
    for g in groups:
        slot = ROWS * g + tile
        if slot < SLOTS:
            v = roll(ref[pl.ds(row_of(slot), SIDE, stride=stride), :], GAP * g)
            inside = (lane >= GAP * g) & (lane < GAP * g + SIDE)
            acc = jnp.where(inside, v, acc)
    return acc


def filter_step(src, dst, coef, first):
    lane = lanes((SIDE, LANE))
    inside = (lane < 3 * GAP) & (lane % GAP < SIDE)
    scale = (0.5 if first else 1.0) / HALF_WIDTH
    beta = jnp.where(inside, scale, 0.0).astype(F32)
    for r in range(ROWS):
        c = src[r, 8:48, :]
        if r == 0:
            below = jnp.where(lane >= GAP, roll(src[ROWS - 1, 8:48, :], GAP), 0.0)
        else:
            below = src[r - 1, 8:48, :]
        if r == ROWS - 1:
            above = roll(src[0, 8:48, :], -GAP)
        else:
            above = src[r + 1, 8:48, :]
        near = (below + above) + (src[r, 7:47, :] + src[r, 9:49, :])
        near = near + (roll(c, 1) + roll(c, -1))
        if first:
            dst[r, 8:48, :] = (0.5 * coef[r]) * c - beta * near
        else:
            dst[r, 8:48, :] = coef[r] * c - beta * near - dst[r, 8:48, :]


def chebyshev(buf_a, buf_b, coef):
    filter_step(buf_a, buf_b, coef, True)
    filter_step(buf_b, buf_a, coef, False)

    def two(_, carry):
        filter_step(buf_a, buf_b, coef, False)
        filter_step(buf_b, buf_a, coef, False)
        return carry

    lax.fori_loop(0, (DEG - 2) // 2, two, 0)


def clear_edges(buf):
    zero = jnp.zeros((8, LANE), F32)
    for r in range(ROWS):
        buf[r, 0:8, :] = zero
        buf[r, 48:56, :] = zero


def place():
    dom = lax.axis_index("dom")
    band = lax.axis_index("band")
    xi = lax.rem(band, 4)
    zi = lax.rem(band // 4, 16)
    yh = band // 64
    return dom, band, xi, zi, yh


def main_kernel(
    offs_in, psi, pot, *rest
):
    sources, rest = rest[:TABLES], rest[TABLES:]
    field, coef_out, *rest = rest
    copies, rest = rest[:TABLES], rest[TABLES:]
    lam2, lam_y, by, cz, cx, xall, zt, yt = copies
    (
    offs, psi_raw, pot_raw, in_sems, psi_pad, pot_pad, lines, pot_lines, h_pad, h_recv, buf_a, buf_b, coef, squares,
    p_send, x_recv, y_send, y_recv, z_send, z_recv, z_all, c_send, c_recv, f_recv, h2_recv,
    ready2, ready3, h_sems, h2_sems, xs, xr, ys, yr, zs, zr, as_, ar, cs, cr, fs, fr,
    ) = rest
    loads = [
        pltpu.make_async_copy(a, b, in_sems.at[n])
        for n, (a, b) in enumerate(zip((psi, pot, offs_in, *sources), (psi_raw, pot_raw, offs, *copies)))
    ]
    dom, band, xi, zi, yh = place()
    yc = yh * 8 + dom
    s = lax.rem(xi, 2)
    partner = xi + 1 - 2 * s

    def at_x(x):
        return (dom, band - xi + x)

    def at_z(z):
        return (dom, yh * 64 + z * 4 + xi)

    def at_y(c):
        high = jnp.where(c >= 8, 1, 0)
        return (c - 8 * high, high * 64 + zi * 4 + xi)

    def turn(value, n):
        return jnp.where(value >= n, value - n, value)

    barrier = pltpu.get_barrier_semaphore()
    def signal(sem, to):
        pl.semaphore_signal(sem, inc=1, device_id=to, device_id_type=MESH)

    core = lax.rem(dom, 2)
    other = 1 - 2 * core

    def at_y_near(lines, flip):
        return at_y(turn(turn(yc + 2 * lines + 16, 16), 16) + flip * other)

    for o in (2, 14, 1, 15):
        signal(barrier, at_z(turn(zi + o, 16)))
    for o in (2, 1, 3):
        signal(barrier, at_x(turn(xi + o, 4)))
    for n in (-1, 1):
        signal(barrier, at_y_near(n, 0))
        signal(barrier, at_y_near(n, 1))
    signal(barrier, at_y_near(0, 1))
    for load in loads:
        load.start()
    pl.semaphore_wait(barrier, 12)

    halo = pltpu.make_async_remote_copy(
        src_ref=psi.at[pl.ds(12 - 12 * s, HALO)], dst_ref=h_recv, send_sem=h_sems.at[0], recv_sem=h_sems.at[1],
        device_id=at_x(partner), device_id_type=MESH,
    )
    halo.start()
    for o in (2, 14):
        signal(ready2, at_z(turn(zi + o, 16)))
    for n in (-1, 1):
        signal(ready2, at_y_near(n, 0))

    clear_edges(buf_a)
    clear_edges(buf_b)
    loads[0].wait()
    psi_pad[0:20, 0:1600] = psi_raw[...].reshape(20, 1600)

    def row_of(slot):
        if slot < 20:
            return 8 + slot + s * (19 - 2 * slot)
        return (slot - 20) + s * (47 - 2 * slot)

    for y in range(SIDE):
        lines[y * 32 + 8 : y * 32 + 32, :] = line_of(psi_pad, 24, y)
    for r in range(ROWS):
        buf_a[r, 8:48, :] = to_tiles(lines, 32, row_of, r, (0, 1))
    loads[1].wait()
    pot_pad[:, 0:1600] = pot_raw[...]
    for y in range(SIDE):
        pot_lines[y * 40 : y * 40 + 40, :] = line_of(pot_pad, 40, y)
    for r in range(ROWS):
        coef[r] = to_tiles(
            pot_lines, 40, lambda slot: slot + s * (39 - 2 * slot), r
        ) * (2.0 / HALF_WIDTH)
    for load in loads[2:]:
        load.wait()
    pl.semaphore_wait(ready2, 4)
    for o in (4, 12):
        signal(ready3, at_z(turn(zi + o, 16)))
    for n in (-2, 2):
        signal(ready3, at_y_near(n, 0))
    halo.wait()
    h_pad[:, 0:1600] = h_recv[...].reshape(HALO, 1600)
    for y in range(SIDE):
        lines[y * 32 : y * 32 + 8, :] = line_of(h_pad, 8, y)
    for r in range(HALO):
        buf_a[r, 8:48, :] = to_tiles(lines, 32, row_of, r, (2,), buf_a[r, 8:48, :])
    chebyshev(buf_a, buf_b, coef)

    lane32 = lanes((32, LANE))
    for t in range(4):
        acc = jnp.zeros((32, LANE), F32)
        for q in range(4):
            g, r = divmod(BUF + 4 * t + q, ROWS)
            v = roll(buf_a[r, 12:44, :], 32 * q - GAP * g - BUF)
            acc = jnp.where(lane32 // 32 == q, v, acc)
        squares[:, t * LANE : (t + 1) * LANE] = acc * acc * (1.0 / 64.0)

    corners = 1.0 - offs[...].astype(F32) * (1.0 / 16.0)

    def sign(d, axis):
        return corners[axis : axis + 1, d : d + 1]

    own_dom = lax.broadcasted_iota(jnp.int32, (1, 8), 1) == dom
    sign_y = jnp.sum(jnp.where(own_dom, corners[1:2], 0.0), axis=1, keepdims=True)
    odd_row = lax.broadcasted_iota(jnp.int32, (GRID, 32), 0) >= 32
    parts = dot(jnp.where(odd_row, sign_y, 1.0) * by[...], squares[...])
    for x in range(4):
        p_send[x] = parts[16 * x : 16 * x + 16]

    def x_copy(x, slot):
        return pltpu.make_async_remote_copy(
            src_ref=p_send.at[x], dst_ref=x_recv.at[slot], send_sem=xs.at[x],
            recv_sem=xr.at[slot], device_id=at_x(x), device_id_type=MESH,
        )

    for o in (2, 1, 3):
        x_copy(turn(xi + o, 4), xi).start()
    x_recv[xi] = p_send[xi]
    halo2 = pltpu.make_async_remote_copy(
        src_ref=buf_a.at[2:10, 8:48, :], dst_ref=h2_recv, send_sem=h2_sems.at[0],
        recv_sem=h2_sems.at[1], device_id=at_x(partner), device_id_type=MESH,
    )
    halo2.start()
    for o in (1, 3, 2):
        x_copy(turn(xi + o, 4), turn(xi - o + 4, 4)).wait_recv()
    for h in range(2):
        both = x_recv[h] + x_recv[h + 2]
        for t in range(4):
            y_send[pl.ds(h * 4 + t, 16, stride=8), :] = both[:, t * LANE : (t + 1) * LANE]

    def rows(index, size):
        return pl.ds(pl.multiple_of(index * size, 8), size)

    def y_copy(c, slot):
        return pltpu.make_async_remote_copy(
            src_ref=y_send.at[rows(c, 8)], dst_ref=y_recv.at[rows(slot, 8)], send_sem=ys,
            recv_sem=yr, device_id=at_y(c), device_id_type=MESH,
        )

    def whole(ref, send_sem, recv_sem):
        return pltpu.make_async_remote_copy(
            src_ref=ref, dst_ref=ref, send_sem=send_sem, recv_sem=recv_sem,
            device_id=at_x(partner), device_id_type=MESH,
        )

    y_whole = whole(y_recv.at[0:120], ys, yr)
    f_whole = whole(f_recv.at[0 : 48 * USED], fs, fr)

    pl.semaphore_wait(ready3, 4)
    for o in FAR:
        y_copy(turn(yc + o, 16), yc).start()
    y_recv[rows(yc, 8), :] = y_send[rows(yc, 8), :]
    y_whole.wait_recv()

    d_all = y_recv[0:64, :] + y_recv[64:128, :]
    lane64 = lanes((64, LANE))
    masked = jnp.concatenate([jnp.where(lane64 // 32 == q, d_all, 0.0) for q in range(4)], 0)
    v_all = dot(masked, cz[...])
    lane8 = lanes((8, LANE))
    signs = []
    for d in range(8):
        sign_z = jnp.where(lane8 % 64 >= 32, sign(d, 2), 1.0)
        signs.append(sign_z * jnp.where(lane8 >= 64, sign(d, 0), 1.0))
    v_all = v_all * jnp.concatenate(signs * 4, 0)
    o_all = dot(cx[...], v_all)
    lane_r = lanes((32, LANE))
    left = lane_r < 64
    r2 = jnp.where(left, o_all[0:32], o_all[32:64])
    z_send[...] = r2

    tile_of = zi - FIRST_SUM
    sums = zi >= FIRST_SUM

    def z_copy(t, slot):
        return pltpu.make_async_remote_copy(
            src_ref=z_send.at[8 * t : 8 * t + 8], dst_ref=z_recv.at[rows(slot, 8)], send_sem=zs,
            recv_sem=zr, device_id=at_z(FIRST_SUM + t), device_id_type=MESH,
        )

    for t in range(4):

        @pl.when(zi != FIRST_SUM + t)
        def _():
            z_copy(t, zi).start()

    @pl.when(sums)
    def _():
        z_recv[rows(zi, 8), :] = z_send[rows(tile_of, 8), :]
        whole(z_recv.at[0:120], zs, zr).wait_recv()
        total = z_recv[0:8]
        for k in range(1, 16):
            total = total + z_recv[8 * k : 8 * k + 8]
        z_all[rows(tile_of, 8), :] = total
        for z in SUM_TO:

            @pl.when(zi != z)
            def _():
                pltpu.make_async_remote_copy(
                    src_ref=z_all.at[rows(tile_of, 8)], dst_ref=z_all.at[rows(tile_of, 8)],
                    send_sem=as_, recv_sem=ar, device_id=at_z(z), device_id_type=MESH,
                ).start()

        whole(z_all.at[0:24], as_, ar).wait_recv()

    @pl.when(zi < FIRST_SUM)
    def _():
        whole(z_all.at[0:32], as_, ar).wait_recv()

    r2 = z_all[...]
    lam = lam2[...] + lam_y[pl.ds(xi * 16 + yc, 1), :]
    factor = jnp.where(lam == 0.0, 0.0, 4.0 * math.pi / jnp.where(lam == 0.0, 1.0, lam))
    phi2 = r2 * factor
    top = jnp.where(left, r2, roll(phi2, 64))
    bottom = jnp.where(left, roll(r2, 64), phi2)
    t_all = dot(xall[...], jnp.concatenate([top, bottom], 0))
    t0, t1, t2 = t_all[0:40], t_all[40:80], t_all[80:120]
    left40 = lanes((40, LANE)) < 64
    of_rho = jnp.concatenate([jnp.where(left40, t0, roll(t1, 64)), t2], 1)
    of_phi = jnp.concatenate([jnp.where(left40, roll(t0, 64), t1), roll(t2, 64)], 1)
    planes = dot(jnp.concatenate([of_rho, of_phi], 0), zt[...])
    for d in range(8):
        both = planes[:, 0:LANE] + sign(d, 2) * planes[:, LANE : 2 * LANE]
        for f in range(2):
            rows20 = both[40 * f : 40 * f + 20] + sign(d, 0) * both[40 * f + 20 : 40 * f + 40]
            for h in range(2):
                at = (2 * d + h) * PART + 10 * f
                c_send[at : at + 10, :] = rows20[10 * h : 10 * h + 10]

    def used(index):
        return pl.ds(pl.multiple_of(index * PART, 8), USED)

    def c_copy(c, slot, h):
        return pltpu.make_async_remote_copy(
            src_ref=c_send.at[used(2 * (c - jnp.where(c >= 8, 8, 0)) + h)],
            dst_ref=c_recv.at[used(2 * slot + h)], send_sem=cs,
            recv_sem=cr.at[slot], device_id=at_y(c), device_id_type=MESH,
        )

    for o in NEAR:
        for h in range(2):
            c_copy(turn(yc + o, 16), yc, h).start()
    c_recv[rows(yc, 2 * PART), :] = c_send[rows(dom, 2 * PART), :]

    def f_copy(x, h, c, from_x):
        return pltpu.make_async_remote_copy(
            src_ref=c_recv.at[used(2 * c + h)],
            dst_ref=f_recv.at[used(from_x * 16 + c)],
            send_sem=fs, recv_sem=fr,
            device_id=at_x(x), device_id_type=MESH,
        )

    def forward(c):
        for o in (2, 1, 3):
            f_copy(turn(xi + o, 4), s if o == 2 else 1 - s, c, xi).start()
        f_recv[rows(xi * 16 + c, PART), :] = c_recv[rows(2 * c + s, PART), :]

    forward(yc)

    y_whole.wait_send()

    @pl.when(sums)
    def _():
        whole(z_send.at[0:24], zs, zr).wait_send()
        whole(z_recv.at[0:120], as_, ar).wait_send()

    @pl.when(zi < FIRST_SUM)
    def _():
        whole(z_send.at[0:32], zs, zr).wait_send()

    for o in range(1, 4):
        x_copy(turn(xi + o, 4), xi).wait_send()

    for o in NEAR:
        c = turn(yc - o + 16, 16)
        whole(c_recv.at[0 : 2 * USED], cs, cr.at[c]).wait_recv()
        forward(c)

    halo2.wait()
    lane40 = lanes((SIDE, LANE))
    for r in range(ROWS):
        own = jnp.where(lane40 < 2 * GAP, buf_a[r, 8:48, :], 0.0)
        if r < HALO:
            inside = (lane40 >= 2 * GAP) & (lane40 < 2 * GAP + SIDE)
            own = jnp.where(inside, roll(h2_recv[HALO - 1 - r], GAP), own)
        field[r] = own

    f_whole.wait_recv()

    odd_col = lanes((SIDE, GRID)) >= 32
    to_y = jnp.where(odd_col, sign_y, 1.0) * yt[...]
    for r in range(ROWS):
        rho = dot(to_y, f_recv[pl.ds(r, GRID, stride=PART), :])
        phi = dot(to_y, f_recv[pl.ds(ROWS + r, GRID, stride=PART), :])
        coef_out[r] = coef[r] + (phi + EXCHANGE * cbrt(rho)) * (2.0 / HALF_WIDTH)
    whole(c_recv.at[0 : 30 * USED], cs, cs).wait_send()
    f_whole.wait_send()


def last_kernel(field, coef, out, buf_a, buf_b, lines):
    band = lax.axis_index("band")
    s = lax.rem(band, 2)
    clear_edges(buf_a)
    clear_edges(buf_b)
    for r in range(ROWS):
        buf_a[r, 8:48, :] = field[r]
    chebyshev(buf_a, buf_b, coef)
    for slot in range(20):
        g, r = divmod(slot, ROWS)
        row = slot + s * (19 - 2 * slot)
        lines[pl.ds(row, SIDE, stride=24), :] = roll(buf_a[r, 8:48, :], -GAP * g)
    lane = lanes((24, LANE))
    for block in range(13):
        acc = jnp.zeros((24, LANE), F32)
        for y in range(SIDE):
            start = SIDE * y - LANE * block
            if start + SIDE > 0 and start < LANE:
                v = roll(lines[y * 24 : y * 24 + 24, :], start)
                inside = (lane >= start) & (lane < start + SIDE)
                acc = jnp.where(inside, v, acc)
        width = min(LANE, 1600 - LANE * block)
        for x in range(20):
            out[x, :, block * LANE : block * LANE + width] = acc[x : x + 1, 0:width]


def local(psi_in, v_in, offsets):
    consts = tables()
    vmem = pl.BlockSpec(memory_space=pltpu.VMEM)
    dma = pltpu.SemaphoreType.DMA
    tile = jax.ShapeDtypeStruct((ROWS, SIDE, LANE), F32)

    def scratch(*shape):
        return pltpu.VMEM(shape, F32)

    operands = (
        offsets.T, jnp.swapaxes(psi_in[0], 0, 1), v_in[0], *[jnp.asarray(a) for a in consts]
    )
    field, coef = pl.pallas_call(
        main_kernel,
        out_shape=(tile, tile),
        in_specs=[pl.BlockSpec(memory_space=pltpu.HBM)] * (3 + TABLES),
        out_specs=(vmem, vmem),
        scratch_shapes=[
            *[scratch(*a.shape) for a in consts], pltpu.VMEM((3, 8), jnp.int32),
            scratch(20, 1, 1600), scratch(40, 1600), dma((3 + TABLES,)),
            scratch(24, 1664), scratch(40, 1664), scratch(40 * 32, LANE), scratch(40 * 40, LANE),
            scratch(8, 1664), scratch(HALO, 1, 1600), scratch(ROWS, 56, LANE), scratch(ROWS, 56, LANE),
            scratch(ROWS, SIDE, LANE), scratch(32, 512),
            scratch(4, 16, 512), scratch(4, 16, 512), scratch(128, LANE), scratch(128, LANE),
            scratch(32, LANE), scratch(128, LANE), scratch(32, LANE),
            scratch(16 * PART, LANE), scratch(32 * PART, LANE), scratch(64 * PART, LANE),
            scratch(HALO, SIDE, LANE),
            pltpu.SemaphoreType.REGULAR, pltpu.SemaphoreType.REGULAR,
            dma((2,)), dma((2,)), dma((4,)), dma((4,)), dma, dma, dma, dma, dma, dma,
            dma, dma((16,)), dma, dma,
        ],
        compiler_params=pltpu.CompilerParams(collective_id=0, has_side_effects=True, vmem_limit_bytes=24 << 20
        ),
        name="step",
    )(*[pltpu.with_memory_space_constraint(a, pltpu.HBM) for a in operands])
    out = pl.pallas_call(
        last_kernel,
        out_shape=jax.ShapeDtypeStruct((20, 1, 1600), F32),
        in_specs=[vmem, vmem],
        out_specs=vmem,
        scratch_shapes=[
            scratch(ROWS, 56, LANE), scratch(ROWS, 56, LANE), scratch(40 * 24, LANE),
        ],
        compiler_params=pltpu.CompilerParams(vmem_limit_bytes=8 << 20),
        name="last",
    )(field, coef)
    return jnp.swapaxes(out, 0, 1)[None]


def solution(mesh):
    return jax.shard_map(
        local,
        mesh=mesh,
        in_specs=(P("dom", "band", None, None), P("dom", None, None), P()),
        out_specs=P("dom", "band", None, None),
        check_vma=False,
    )
```

```python
import functools
import math

import jax
import jax.numpy as jnp
import numpy as np
from jax import lax
from jax.experimental import pallas as pl
from jax.experimental.pallas import tpu as pltpu
from jax.sharding import PartitionSpec as P

F32 = jnp.float32
MESH = pl.DeviceIdType.MESH
GRID = 64
SIDE = 40
BUF = 4
LANE = 128
GAP = 42
ROWS = 10
SLOTS = 28
HALO = 8
DEG = 8
HALF_WIDTH = 4.5
EXCHANGE = -((3.0 / math.pi) ** (1.0 / 3.0))
PART = 24
USED = 20
TABLES = 8
NEAR = [o for m in range(1, 8) for o in (m, 16 - m)] + [8]
FAR = NEAR[::-1]
FIRST_SUM = 12
SUM_TO = (0, 1, 2, 3, 4, 11, 5, 10, 6, 9, 7, 8, 12, 13, 14, 15)


def wave_list():
    even = [("c", k) for k in range(0, 33, 2)] + [("s", k) for k in range(2, 32, 2)]
    odd = [("c", k) for k in range(1, 32, 2)] + [("s", k) for k in range(1, 32, 2)]
    return even + odd


def basis(cells):
    cells = np.asarray(cells, np.float64)
    rows = []
    for kind, k in wave_list():
        angle = 2.0 * np.pi * k * cells / GRID
        size = 1.0 if k in (0, 32) else 2.0
        rows.append(np.sqrt(size / GRID) * (np.cos(angle) if kind == "c" else np.sin(angle)))
    return np.stack(rows)


def tables():
    waves = np.array([k for _, k in wave_list()])
    lam = 2.0 - 2.0 * np.cos(2.0 * np.pi * waves / GRID)
    by = basis(np.arange(32))
    cz = np.tile(basis(np.arange(32)).T, (4, 2))
    cx = np.zeros((GRID, 4, 8, 2, 4))
    for q in range(4):
        for s in range(2):
            for t in range(4):
                n = 4 * t + q
                cx[:, q, :, s, t] = basis([n if s == 0 else 31 - n])
    cx = cx.reshape(GRID, 256)
    xall = np.zeros((3, 2, 2, ROWS, GRID))
    for g in range(3):
        for s in range(2):
            for r in range(ROWS):
                slot = ROWS * g + r
                if slot < SLOTS:
                    wave = basis([slot - BUF if s == 0 else 35 - slot])[:, 0]
                    xall[g, 0, s, r, :32] = wave[:32]
                    xall[g, 1, s, r, 32:] = wave[32:]
    xall = xall.reshape(120, GRID)
    zt = np.zeros((256, 2, LANE))
    region = basis(np.arange(SIDE) - BUF)
    for g in range(3):
        for b in range(2):
            zt[64 * g + 32 * b : 64 * g + 32 * b + 32, b, GAP * g : GAP * g + SIDE] = region[
                32 * b : 32 * b + 32
            ]
    zt = zt.reshape(256, 256)
    yt = region.T
    lam2 = np.concatenate(
        [lam[:32, None] + lam[None, :], lam[32:, None] + lam[None, :]], axis=1
    )
    lam_y = np.repeat(lam[:, None], LANE, axis=1)
    out = (lam2, lam_y, by, cz, cx, xall, zt, yt)
    return [np.asarray(a, np.float32) for a in out]


def lanes(shape):
    return lax.broadcasted_iota(jnp.int32, shape, len(shape) - 1)


def dot(a, b):
    return jnp.dot(a, b, precision=lax.Precision.HIGHEST, preferred_element_type=F32)


def roll(v, shift):
    shift %= LANE
    return v if shift == 0 else pltpu.roll(v, shift, 1)


def cbrt(x):
    a = jnp.abs(x)
    tiny = 1.2e-38
    b = jnp.maximum(a, tiny)
    y = jnp.exp(jnp.log(b) * (1.0 / 3.0))
    y = y - (y - b / (y * y)) * (1.0 / 3.0)
    y = jnp.where(a < tiny, 0.0, y)
    return jnp.where(x < 0.0, -y, y)


def line_of(ref, rows, y):
    block, at = divmod(SIDE * y, LANE)
    v = roll(ref[0:rows, block * LANE : (block + 1) * LANE], -at)
    if at + SIDE > LANE:
        w = roll(ref[0:rows, (block + 1) * LANE : (block + 2) * LANE], -at)
        v = jnp.where(lanes(v.shape) < LANE - at, v, w)
    return v


def to_tiles(ref, stride, row_of, tile, groups=(0, 1, 2), acc=None):
    lane = lanes((SIDE, LANE))
    if acc is None:
        acc = jnp.zeros((SIDE, LANE), F32)
    for g in groups:
        slot = ROWS * g + tile
        if slot < SLOTS:
            v = roll(ref[pl.ds(row_of(slot), SIDE, stride=stride), :], GAP * g)
            inside = (lane >= GAP * g) & (lane < GAP * g + SIDE)
            acc = jnp.where(inside, v, acc)
    return acc


def filter_step(src, dst, coef, number):
    first = number == 0
    lane = lanes((SIDE, LANE))
    inside = (lane < 3 * GAP) & (lane % GAP < SIDE)
    scale = (0.5 if first else 1.0) / HALF_WIDTH
    beta = jnp.where(inside, scale, 0.0).astype(F32)
    for r in [(number + n) % ROWS for n in range(ROWS)]:
        c = src[r, 8:48, :]
        if r == 0:
            below = jnp.where(lane >= GAP, roll(src[ROWS - 1, 8:48, :], GAP), 0.0)
        else:
            below = src[r - 1, 8:48, :]
        if r == ROWS - 1:
            above = roll(src[0, 8:48, :], -GAP)
        else:
            above = src[r + 1, 8:48, :]
        near = (below + above) + (src[r, 7:47, :] + src[r, 9:49, :])
        near = near + (roll(c, 1) + roll(c, -1))
        if first:
            dst[r, 8:48, :] = (0.5 * coef[r]) * c - beta * near
        else:
            dst[r, 8:48, :] = coef[r] * c - beta * near - dst[r, 8:48, :]


def chebyshev(buf_a, buf_b, coef):
    for number in range(DEG):
        src, dst = (buf_a, buf_b) if number % 2 == 0 else (buf_b, buf_a)
        filter_step(src, dst, coef, number)


def clear_edges(buf):
    zero = jnp.zeros((8, LANE), F32)
    for r in range(ROWS):
        buf[r, 0:8, :] = zero
        buf[r, 48:56, :] = zero


def place():
    dom = lax.axis_index("dom")
    band = lax.axis_index("band")
    xi = lax.rem(band, 4)
    zi = lax.rem(band // 4, 16)
    yh = band // 64
    return dom, band, xi, zi, yh


def main_kernel(
    offs_in, psi, pot, *rest
):
    sources, rest = rest[:TABLES], rest[TABLES:]
    field, coef_out, *rest = rest
    copies, rest = rest[:TABLES], rest[TABLES:]
    lam2, lam_y, by, cz, cx, xall, zt, yt = copies
    (
    offs, psi_raw, pot_raw, in_sems, psi_pad, pot_pad, lines, pot_lines, h_pad, h_recv, buf_a, buf_b, coef, squares,
    p_send, x_recv, y_send, y_recv, z_send, z_recv, z_all, c_send, c_recv, f_recv, h2_recv,
    ready2, ready3, h_sems, h2_sems, xs, xr, ys, yr, zs, zr, as_, ar, cs, cr, fs, fr,
    ) = rest
    loads = [
        pltpu.make_async_copy(a, b, in_sems.at[n])
        for n, (a, b) in enumerate(zip((psi, pot, offs_in, *sources), (psi_raw, pot_raw, offs, *copies)))
    ]
    dom, band, xi, zi, yh = place()
    yc = yh * 8 + dom
    s = lax.rem(xi, 2)
    partner = xi + 1 - 2 * s

    def at_x(x):
        return (dom, band - xi + x)

    def at_z(z):
        return (dom, yh * 64 + z * 4 + xi)

    def at_y(c):
        high = jnp.where(c >= 8, 1, 0)
        return (c - 8 * high, high * 64 + zi * 4 + xi)

    def turn(value, n):
        return jnp.where(value >= n, value - n, value)

    barrier = pltpu.get_barrier_semaphore()
    def signal(sem, to):
        pl.semaphore_signal(sem, inc=1, device_id=to, device_id_type=MESH)

    core = lax.rem(dom, 2)
    other = 1 - 2 * core

    def at_y_near(lines, flip):
        return at_y(turn(turn(yc + 2 * lines + 16, 16), 16) + flip * other)

    for o in (2, 14, 1, 15):
        signal(barrier, at_z(turn(zi + o, 16)))
    for o in (2, 1, 3):
        signal(barrier, at_x(turn(xi + o, 4)))
    for n in (-1, 1):
        signal(barrier, at_y_near(n, 0))
        signal(barrier, at_y_near(n, 1))
    signal(barrier, at_y_near(0, 1))
    for load in loads:
        load.start()
    pl.semaphore_wait(barrier, 12)

    halo = pltpu.make_async_remote_copy(
        src_ref=psi.at[pl.ds(12 - 12 * s, HALO)], dst_ref=h_recv, send_sem=h_sems.at[0], recv_sem=h_sems.at[1],
        device_id=at_x(partner), device_id_type=MESH,
    )
    halo.start()
    for o in (2, 14):
        signal(ready2, at_z(turn(zi + o, 16)))
    for n in (-1, 1):
        signal(ready2, at_y_near(n, 0))

    clear_edges(buf_a)
    clear_edges(buf_b)
    loads[0].wait()
    psi_pad[0:20, 0:1600] = psi_raw[...].reshape(20, 1600)

    def row_of(slot):
        if slot < 20:
            return 8 + slot + s * (19 - 2 * slot)
        return (slot - 20) + s * (47 - 2 * slot)

    for y in range(SIDE):
        lines[y * 32 + 8 : y * 32 + 32, :] = line_of(psi_pad, 24, y)
    for r in range(ROWS):
        buf_a[r, 8:48, :] = to_tiles(lines, 32, row_of, r, (0, 1))
    loads[1].wait()
    pot_pad[:, 0:1600] = pot_raw[...]
    for y in range(SIDE):
        pot_lines[y * 40 : y * 40 + 40, :] = line_of(pot_pad, 40, y)
    for r in range(ROWS):
        coef[r] = to_tiles(
            pot_lines, 40, lambda slot: slot + s * (39 - 2 * slot), r
        ) * (2.0 / HALF_WIDTH)
    for load in loads[2:]:
        load.wait()
    pl.semaphore_wait(ready2, 4)
    for o in (4, 12):
        signal(ready3, at_z(turn(zi + o, 16)))
    for n in (-2, 2):
        signal(ready3, at_y_near(n, 0))
    halo.wait()
    h_pad[:, 0:1600] = h_recv[...].reshape(HALO, 1600)
    for y in range(SIDE):
        lines[y * 32 : y * 32 + 8, :] = line_of(h_pad, 8, y)
    for r in range(HALO):
        buf_a[r, 8:48, :] = to_tiles(lines, 32, row_of, r, (2,), buf_a[r, 8:48, :])
    chebyshev(buf_a, buf_b, coef)

    lane32 = lanes((32, LANE))
    for t in range(4):
        acc = jnp.zeros((32, LANE), F32)
        for q in range(4):
            g, r = divmod(BUF + 4 * t + q, ROWS)
            v = roll(buf_a[r, 12:44, :], 32 * q - GAP * g - BUF)
            acc = jnp.where(lane32 // 32 == q, v, acc)
        squares[:, t * LANE : (t + 1) * LANE] = acc * acc * (1.0 / 64.0)

    corners = 1.0 - offs[...].astype(F32) * (1.0 / 16.0)

    def sign(d, axis):
        return corners[axis : axis + 1, d : d + 1]

    own_dom = lax.broadcasted_iota(jnp.int32, (1, 8), 1) == dom
    sign_y = jnp.sum(jnp.where(own_dom, corners[1:2], 0.0), axis=1, keepdims=True)
    odd_row = lax.broadcasted_iota(jnp.int32, (GRID, 32), 0) >= 32
    parts = dot(jnp.where(odd_row, sign_y, 1.0) * by[...], squares[...])
    for x in range(4):
        p_send[x] = parts[16 * x : 16 * x + 16]

    def x_copy(x, slot):
        return pltpu.make_async_remote_copy(
            src_ref=p_send.at[x], dst_ref=x_recv.at[slot], send_sem=xs.at[x],
            recv_sem=xr.at[slot], device_id=at_x(x), device_id_type=MESH,
        )

    for o in (2, 1, 3):
        x_copy(turn(xi + o, 4), xi).start()
    x_recv[xi] = p_send[xi]
    halo2 = pltpu.make_async_remote_copy(
        src_ref=buf_a.at[2:10, 8:48, :], dst_ref=h2_recv, send_sem=h2_sems.at[0],
        recv_sem=h2_sems.at[1], device_id=at_x(partner), device_id_type=MESH,
    )
    halo2.start()
    for o in (1, 3, 2):
        x_copy(turn(xi + o, 4), turn(xi - o + 4, 4)).wait_recv()
    for h in range(2):
        both = x_recv[h] + x_recv[h + 2]
        for t in range(4):
            y_send[pl.ds(h * 4 + t, 16, stride=8), :] = both[:, t * LANE : (t + 1) * LANE]

    def rows(index, size):
        return pl.ds(pl.multiple_of(index * size, 8), size)

    def y_copy(c, slot):
        return pltpu.make_async_remote_copy(
            src_ref=y_send.at[rows(c, 8)], dst_ref=y_recv.at[rows(slot, 8)], send_sem=ys,
            recv_sem=yr, device_id=at_y(c), device_id_type=MESH,
        )

    def whole(ref, send_sem, recv_sem):
        return pltpu.make_async_remote_copy(
            src_ref=ref, dst_ref=ref, send_sem=send_sem, recv_sem=recv_sem,
            device_id=at_x(partner), device_id_type=MESH,
        )

    y_whole = whole(y_recv.at[0:120], ys, yr)
    f_whole = whole(f_recv.at[0 : 48 * USED], fs, fr)

    pl.semaphore_wait(ready3, 4)
    for o in FAR:
        y_copy(turn(yc + o, 16), yc).start()
    y_recv[rows(yc, 8), :] = y_send[rows(yc, 8), :]
    y_whole.wait_recv()

    d_all = y_recv[0:64, :] + y_recv[64:128, :]
    lane64 = lanes((64, LANE))
    masked = jnp.concatenate([jnp.where(lane64 // 32 == q, d_all, 0.0) for q in range(4)], 0)
    v_all = dot(masked, cz[...])
    lane8 = lanes((8, LANE))
    signs = []
    for d in range(8):
        sign_z = jnp.where(lane8 % 64 >= 32, sign(d, 2), 1.0)
        signs.append(sign_z * jnp.where(lane8 >= 64, sign(d, 0), 1.0))
    v_all = v_all * jnp.concatenate(signs * 4, 0)
    o_all = dot(cx[...], v_all)
    lane_r = lanes((32, LANE))
    left = lane_r < 64
    r2 = jnp.where(left, o_all[0:32], o_all[32:64])
    z_send[...] = r2

    tile_of = zi - FIRST_SUM
    sums = zi >= FIRST_SUM

    def z_copy(t, slot):
        return pltpu.make_async_remote_copy(
            src_ref=z_send.at[8 * t : 8 * t + 8], dst_ref=z_recv.at[rows(slot, 8)], send_sem=zs,
            recv_sem=zr, device_id=at_z(FIRST_SUM + t), device_id_type=MESH,
        )

    for t in range(4):

        @pl.when(zi != FIRST_SUM + t)
        def _():
            z_copy(t, zi).start()

    @pl.when(sums)
    def _():
        z_recv[rows(zi, 8), :] = z_send[rows(tile_of, 8), :]
        whole(z_recv.at[0:120], zs, zr).wait_recv()
        total = z_recv[0:8]
        for k in range(1, 16):
            total = total + z_recv[8 * k : 8 * k + 8]
        z_all[rows(tile_of, 8), :] = total
        for z in SUM_TO:

            @pl.when(zi != z)
            def _():
                pltpu.make_async_remote_copy(
                    src_ref=z_all.at[rows(tile_of, 8)], dst_ref=z_all.at[rows(tile_of, 8)],
                    send_sem=as_, recv_sem=ar, device_id=at_z(z), device_id_type=MESH,
                ).start()

        whole(z_all.at[0:24], as_, ar).wait_recv()

    @pl.when(zi < FIRST_SUM)
    def _():
        whole(z_all.at[0:32], as_, ar).wait_recv()

    r2 = z_all[...]
    lam = lam2[...] + lam_y[pl.ds(xi * 16 + yc, 1), :]
    factor = jnp.where(lam == 0.0, 0.0, 4.0 * math.pi / jnp.where(lam == 0.0, 1.0, lam))
    phi2 = r2 * factor
    top = jnp.where(left, r2, roll(phi2, 64))
    bottom = jnp.where(left, roll(r2, 64), phi2)
    t_all = dot(xall[...], jnp.concatenate([top, bottom], 0))
    t0, t1, t2 = t_all[0:40], t_all[40:80], t_all[80:120]
    left40 = lanes((40, LANE)) < 64
    of_rho = jnp.concatenate([jnp.where(left40, t0, roll(t1, 64)), t2], 1)
    of_phi = jnp.concatenate([jnp.where(left40, roll(t0, 64), t1), roll(t2, 64)], 1)
    planes = dot(jnp.concatenate([of_rho, of_phi], 0), zt[...])
    for d in range(8):
        both = planes[:, 0:LANE] + sign(d, 2) * planes[:, LANE : 2 * LANE]
        for f in range(2):
            rows20 = both[40 * f : 40 * f + 20] + sign(d, 0) * both[40 * f + 20 : 40 * f + 40]
            for h in range(2):
                at = (2 * d + h) * PART + 10 * f
                c_send[at : at + 10, :] = rows20[10 * h : 10 * h + 10]

    def used(index):
        return pl.ds(pl.multiple_of(index * PART, 8), USED)

    def c_copy(c, slot, h):
        return pltpu.make_async_remote_copy(
            src_ref=c_send.at[used(2 * (c - jnp.where(c >= 8, 8, 0)) + h)],
            dst_ref=c_recv.at[used(2 * slot + h)], send_sem=cs,
            recv_sem=cr.at[slot], device_id=at_y(c), device_id_type=MESH,
        )

    for o in NEAR:
        for h in range(2):
            c_copy(turn(yc + o, 16), yc, h).start()
    c_recv[rows(yc, 2 * PART), :] = c_send[rows(dom, 2 * PART), :]

    def f_copy(x, h, c, from_x):
        return pltpu.make_async_remote_copy(
            src_ref=c_recv.at[used(2 * c + h)],
            dst_ref=f_recv.at[used(from_x * 16 + c)],
            send_sem=fs, recv_sem=fr,
            device_id=at_x(x), device_id_type=MESH,
        )

    def forward(c):
        for o in (2, 1, 3):
            f_copy(turn(xi + o, 4), s if o == 2 else 1 - s, c, xi).start()
        f_recv[rows(xi * 16 + c, PART), :] = c_recv[rows(2 * c + s, PART), :]

    forward(yc)

    y_whole.wait_send()

    @pl.when(sums)
    def _():
        whole(z_send.at[0:24], zs, zr).wait_send()
        whole(z_recv.at[0:120], as_, ar).wait_send()

    @pl.when(zi < FIRST_SUM)
    def _():
        whole(z_send.at[0:32], zs, zr).wait_send()

    for o in range(1, 4):
        x_copy(turn(xi + o, 4), xi).wait_send()

    for o in NEAR:
        c = turn(yc - o + 16, 16)
        whole(c_recv.at[0 : 2 * USED], cs, cr.at[c]).wait_recv()
        forward(c)

    halo2.wait()
    lane40 = lanes((SIDE, LANE))
    for r in range(ROWS):
        own = jnp.where(lane40 < 2 * GAP, buf_a[r, 8:48, :], 0.0)
        if r < HALO:
            inside = (lane40 >= 2 * GAP) & (lane40 < 2 * GAP + SIDE)
            own = jnp.where(inside, roll(h2_recv[HALO - 1 - r], GAP), own)
        field[r] = own

    f_whole.wait_recv()

    odd_col = lanes((SIDE, GRID)) >= 32
    to_y = jnp.where(odd_col, sign_y, 1.0) * yt[...]
    for r in range(ROWS):
        rho = dot(to_y, f_recv[pl.ds(r, GRID, stride=PART), :])
        phi = dot(to_y, f_recv[pl.ds(ROWS + r, GRID, stride=PART), :])
        coef_out[r] = coef[r] + (phi + EXCHANGE * cbrt(rho)) * (2.0 / HALF_WIDTH)
    whole(c_recv.at[0 : 30 * USED], cs, cs).wait_send()
    f_whole.wait_send()


def last_kernel(field, coef, out, buf_a, buf_b, lines):
    band = lax.axis_index("band")
    s = lax.rem(band, 2)
    clear_edges(buf_a)
    clear_edges(buf_b)
    for r in range(ROWS):
        buf_a[r, 8:48, :] = field[r]
    chebyshev(buf_a, buf_b, coef)
    for slot in range(20):
        g, r = divmod(slot, ROWS)
        row = slot + s * (19 - 2 * slot)
        lines[pl.ds(row, SIDE, stride=24), :] = roll(buf_a[r, 8:48, :], -GAP * g)
    lane = lanes((24, LANE))
    for block in range(13):
        acc = jnp.zeros((24, LANE), F32)
        for y in range(SIDE):
            start = SIDE * y - LANE * block
            if start + SIDE > 0 and start < LANE:
                v = roll(lines[y * 24 : y * 24 + 24, :], start)
                inside = (lane >= start) & (lane < start + SIDE)
                acc = jnp.where(inside, v, acc)
        width = min(LANE, 1600 - LANE * block)
        for x in range(20):
            out[x, :, block * LANE : block * LANE + width] = acc[x : x + 1, 0:width]


def local(psi_in, v_in, offsets):
    consts = tables()
    vmem = pl.BlockSpec(memory_space=pltpu.VMEM)
    dma = pltpu.SemaphoreType.DMA
    tile = jax.ShapeDtypeStruct((ROWS, SIDE, LANE), F32)

    def scratch(*shape):
        return pltpu.VMEM(shape, F32)

    operands = (
        offsets.T, jnp.swapaxes(psi_in[0], 0, 1), v_in[0], *[jnp.asarray(a) for a in consts]
    )
    field, coef = pl.pallas_call(
        main_kernel,
        out_shape=(tile, tile),
        in_specs=[pl.BlockSpec(memory_space=pltpu.HBM)] * (3 + TABLES),
        out_specs=(vmem, vmem),
        scratch_shapes=[
            *[scratch(*a.shape) for a in consts], pltpu.VMEM((3, 8), jnp.int32),
            scratch(20, 1, 1600), scratch(40, 1600), dma((3 + TABLES,)),
            scratch(24, 1664), scratch(40, 1664), scratch(40 * 32, LANE), scratch(40 * 40, LANE),
            scratch(8, 1664), scratch(HALO, 1, 1600), scratch(ROWS, 56, LANE), scratch(ROWS, 56, LANE),
            scratch(ROWS, SIDE, LANE), scratch(32, 512),
            scratch(4, 16, 512), scratch(4, 16, 512), scratch(128, LANE), scratch(128, LANE),
            scratch(32, LANE), scratch(128, LANE), scratch(32, LANE),
            scratch(16 * PART, LANE), scratch(32 * PART, LANE), scratch(64 * PART, LANE),
            scratch(HALO, SIDE, LANE),
            pltpu.SemaphoreType.REGULAR, pltpu.SemaphoreType.REGULAR,
            dma((2,)), dma((2,)), dma((4,)), dma((4,)), dma, dma, dma, dma, dma, dma,
            dma, dma((16,)), dma, dma,
        ],
        compiler_params=pltpu.CompilerParams(collective_id=0, has_side_effects=True, vmem_limit_bytes=24 << 20
        ),
        name="step",
    )(*[pltpu.with_memory_space_constraint(a, pltpu.HBM) for a in operands])
    out = pl.pallas_call(
        last_kernel,
        out_shape=jax.ShapeDtypeStruct((20, 1, 1600), F32),
        in_specs=[vmem, vmem],
        out_specs=vmem,
        scratch_shapes=[
            scratch(ROWS, 56, LANE), scratch(ROWS, 56, LANE), scratch(40 * 24, LANE),
        ],
        compiler_params=pltpu.CompilerParams(vmem_limit_bytes=8 << 20),
        name="last",
    )(field, coef)
    return jnp.swapaxes(out, 0, 1)[None]


def solution(mesh):
    return jax.shard_map(
        local,
        mesh=mesh,
        in_specs=(P("dom", "band", None, None), P("dom", None, None), P()),
        out_specs=P("dom", "band", None, None),
        check_vma=False,
    )
```

```python
import functools
import math

import jax
import jax.numpy as jnp
import numpy as np
from jax import lax
from jax.experimental import pallas as pl
from jax.experimental.pallas import tpu as pltpu
from jax.sharding import PartitionSpec as P

F32 = jnp.float32
MESH = pl.DeviceIdType.MESH
GRID = 64
SIDE = 40
BUF = 4
LANE = 128
GAP = 42
ROWS = 10
SLOTS = 28
HALO = 8
DEG = 8
HALF_WIDTH = 4.5
EXCHANGE = -((3.0 / math.pi) ** (1.0 / 3.0))
PART = 24
USED = 20
TABLES = 8
NEAR = [o for m in range(1, 8) for o in (m, 16 - m)] + [8]
FAR = NEAR[::-1]
SUMS = (13, 14, 15, 0)
SUM_TO = (0, 1, 2, 3, 4, 5, 6, 11, 7, 10, 8, 9, 12, 13, 14, 15)


def wave_list():
    even = [("c", k) for k in range(0, 33, 2)] + [("s", k) for k in range(2, 32, 2)]
    odd = [("c", k) for k in range(1, 32, 2)] + [("s", k) for k in range(1, 32, 2)]
    return even + odd


def basis(cells):
    cells = np.asarray(cells, np.float64)
    rows = []
    for kind, k in wave_list():
        angle = 2.0 * np.pi * k * cells / GRID
        size = 1.0 if k in (0, 32) else 2.0
        rows.append(np.sqrt(size / GRID) * (np.cos(angle) if kind == "c" else np.sin(angle)))
    return np.stack(rows)


def tables():
    waves = np.array([k for _, k in wave_list()])
    lam = 2.0 - 2.0 * np.cos(2.0 * np.pi * waves / GRID)
    by = basis(np.arange(32))
    cz = np.tile(basis(np.arange(32)).T, (4, 2))
    cx = np.zeros((GRID, 4, 8, 2, 4))
    for q in range(4):
        for s in range(2):
            for t in range(4):
                n = 4 * t + q
                cx[:, q, :, s, t] = basis([n if s == 0 else 31 - n])
    cx = cx.reshape(GRID, 256)
    xall = np.zeros((3, 2, 2, ROWS, GRID))
    for g in range(3):
        for s in range(2):
            for r in range(ROWS):
                slot = ROWS * g + r
                if slot < SLOTS:
                    wave = basis([slot - BUF if s == 0 else 35 - slot])[:, 0]
                    xall[g, 0, s, r, :32] = wave[:32]
                    xall[g, 1, s, r, 32:] = wave[32:]
    xall = xall.reshape(120, GRID)
    zt = np.zeros((256, 2, LANE))
    region = basis(np.arange(SIDE) - BUF)
    for g in range(3):
        for b in range(2):
            zt[64 * g + 32 * b : 64 * g + 32 * b + 32, b, GAP * g : GAP * g + SIDE] = region[
                32 * b : 32 * b + 32
            ]
    zt = zt.reshape(256, 256)
    yt = region.T
    lam2 = np.concatenate(
        [lam[:32, None] + lam[None, :], lam[32:, None] + lam[None, :]], axis=1
    )
    lam_y = np.repeat(lam[:, None], LANE, axis=1)
    out = (lam2, lam_y, by, cz, cx, xall, zt, yt)
    return [np.asarray(a, np.float32) for a in out]


def lanes(shape):
    return lax.broadcasted_iota(jnp.int32, shape, len(shape) - 1)


def dot(a, b):
    return jnp.dot(a, b, precision=lax.Precision.HIGHEST, preferred_element_type=F32)


def roll(v, shift):
    shift %= LANE
    return v if shift == 0 else pltpu.roll(v, shift, 1)


def cbrt(x):
    a = jnp.abs(x)
    tiny = 1.2e-38
    b = jnp.maximum(a, tiny)
    y = jnp.exp(jnp.log(b) * (1.0 / 3.0))
    y = y - (y - b / (y * y)) * (1.0 / 3.0)
    y = jnp.where(a < tiny, 0.0, y)
    return jnp.where(x < 0.0, -y, y)


def line_of(ref, rows, y):
    block, at = divmod(SIDE * y, LANE)
    v = roll(ref[0:rows, block * LANE : (block + 1) * LANE], -at)
    if at + SIDE > LANE:
        w = roll(ref[0:rows, (block + 1) * LANE : (block + 2) * LANE], -at)
        v = jnp.where(lanes(v.shape) < LANE - at, v, w)
    return v


def to_tiles(ref, stride, row_of, tile, groups=(0, 1, 2), acc=None):
    lane = lanes((SIDE, LANE))
    if acc is None:
        acc = jnp.zeros((SIDE, LANE), F32)
    for g in groups:
        slot = ROWS * g + tile
        if slot < SLOTS:
            v = roll(ref[pl.ds(row_of(slot), SIDE, stride=stride), :], GAP * g)
            inside = (lane >= GAP * g) & (lane < GAP * g + SIDE)
            acc = jnp.where(inside, v, acc)
    return acc


def filter_step(src, dst, coef, number):
    first = number == 0
    lane = lanes((SIDE, LANE))
    inside = (lane < 3 * GAP) & (lane % GAP < SIDE)
    scale = (0.5 if first else 1.0) / HALF_WIDTH
    beta = jnp.where(inside, scale, 0.0).astype(F32)
    for r in [(number + n) % ROWS for n in range(ROWS)]:
        c = src[r, 8:48, :]
        if r == 0:
            below = jnp.where(lane >= GAP, roll(src[ROWS - 1, 8:48, :], GAP), 0.0)
        else:
            below = src[r - 1, 8:48, :]
        if r == ROWS - 1:
            above = roll(src[0, 8:48, :], -GAP)
        else:
            above = src[r + 1, 8:48, :]
        near = (below + above) + (src[r, 7:47, :] + src[r, 9:49, :])
        near = near + (roll(c, 1) + roll(c, -1))
        if first:
            dst[r, 8:48, :] = (0.5 * coef[r]) * c - beta * near
        else:
            dst[r, 8:48, :] = coef[r] * c - beta * near - dst[r, 8:48, :]


def chebyshev(buf_a, buf_b, coef):
    for number in range(DEG):
        src, dst = (buf_a, buf_b) if number % 2 == 0 else (buf_b, buf_a)
        filter_step(src, dst, coef, number)


def clear_edges(buf):
    zero = jnp.zeros((8, LANE), F32)
    for r in range(ROWS):
        buf[r, 0:8, :] = zero
        buf[r, 48:56, :] = zero


def place():
    dom = lax.axis_index("dom")
    band = lax.axis_index("band")
    xi = lax.rem(band, 4)
    zi = lax.rem(band // 4, 16)
    yh = band // 64
    return dom, band, xi, zi, yh


def main_kernel(
    offs_in, psi, pot, *rest
):
    sources, rest = rest[:TABLES], rest[TABLES:]
    field, coef_out, *rest = rest
    copies, rest = rest[:TABLES], rest[TABLES:]
    lam2, lam_y, by, cz, cx, xall, zt, yt = copies
    (
    offs, psi_raw, pot_raw, in_sems, psi_pad, pot_pad, lines, pot_lines, h_pad, h_recv, buf_a, buf_b, coef, squares,
    p_send, x_recv, y_send, y_recv, z_send, z_recv, z_all, c_send, c_recv, f_recv, h2_recv,
    ready2, ready3, h_sems, h2_sems, xs, xr, ys, yr, zs, zr, as_, ar, cs, cr, fs, fr,
    ) = rest
    loads = [
        pltpu.make_async_copy(a, b, in_sems.at[n])
        for n, (a, b) in enumerate(zip((psi, pot, offs_in, *sources), (psi_raw, pot_raw, offs, *copies)))
    ]
    dom, band, xi, zi, yh = place()
    yc = yh * 8 + dom
    s = lax.rem(xi, 2)
    partner = xi + 1 - 2 * s

    def at_x(x):
        return (dom, band - xi + x)

    def at_z(z):
        return (dom, yh * 64 + z * 4 + xi)

    def at_y(c):
        high = jnp.where(c >= 8, 1, 0)
        return (c - 8 * high, high * 64 + zi * 4 + xi)

    def turn(value, n):
        return jnp.where(value >= n, value - n, value)

    barrier = pltpu.get_barrier_semaphore()
    def signal(sem, to):
        pl.semaphore_signal(sem, inc=1, device_id=to, device_id_type=MESH)

    core = lax.rem(dom, 2)
    other = 1 - 2 * core

    def at_y_near(lines, flip):
        return at_y(turn(turn(yc + 2 * lines + 16, 16), 16) + flip * other)

    for o in (2, 14, 1, 15):
        signal(barrier, at_z(turn(zi + o, 16)))
    for o in (2, 1, 3):
        signal(barrier, at_x(turn(xi + o, 4)))
    for n in (-1, 1):
        signal(barrier, at_y_near(n, 0))
        signal(barrier, at_y_near(n, 1))
    signal(barrier, at_y_near(0, 1))
    for load in loads:
        load.start()
    pl.semaphore_wait(barrier, 12)

    halo = pltpu.make_async_remote_copy(
        src_ref=psi.at[pl.ds(12 - 12 * s, HALO)], dst_ref=h_recv, send_sem=h_sems.at[0], recv_sem=h_sems.at[1],
        device_id=at_x(partner), device_id_type=MESH,
    )
    halo.start()
    for o in (2, 14):
        signal(ready2, at_z(turn(zi + o, 16)))
    for n in (-1, 1):
        signal(ready2, at_y_near(n, 0))

    clear_edges(buf_a)
    clear_edges(buf_b)
    loads[0].wait()
    psi_pad[0:20, 0:1600] = psi_raw[...].reshape(20, 1600)

    def row_of(slot):
        if slot < 20:
            return 8 + slot + s * (19 - 2 * slot)
        return (slot - 20) + s * (47 - 2 * slot)

    for y in range(SIDE):
        lines[y * 32 + 8 : y * 32 + 32, :] = line_of(psi_pad, 24, y)
    for r in range(ROWS):
        buf_a[r, 8:48, :] = to_tiles(lines, 32, row_of, r, (0, 1))
    loads[1].wait()
    pot_pad[:, 0:1600] = pot_raw[...]
    for y in range(SIDE):
        pot_lines[y * 40 : y * 40 + 40, :] = line_of(pot_pad, 40, y)
    for r in range(ROWS):
        coef[r] = to_tiles(
            pot_lines, 40, lambda slot: slot + s * (39 - 2 * slot), r
        ) * (2.0 / HALF_WIDTH)
    for load in loads[2:]:
        load.wait()
    pl.semaphore_wait(ready2, 4)
    for o in (4, 12):
        signal(ready3, at_z(turn(zi + o, 16)))
    for n in (-2, 2):
        signal(ready3, at_y_near(n, 0))
    halo.wait()
    h_pad[:, 0:1600] = h_recv[...].reshape(HALO, 1600)
    for y in range(SIDE):
        lines[y * 32 : y * 32 + 8, :] = line_of(h_pad, 8, y)
    for r in range(HALO):
        buf_a[r, 8:48, :] = to_tiles(lines, 32, row_of, r, (2,), buf_a[r, 8:48, :])
    chebyshev(buf_a, buf_b, coef)

    lane32 = lanes((32, LANE))
    for t in range(4):
        acc = jnp.zeros((32, LANE), F32)
        for q in range(4):
            g, r = divmod(BUF + 4 * t + q, ROWS)
            v = roll(buf_a[r, 12:44, :], 32 * q - GAP * g - BUF)
            acc = jnp.where(lane32 // 32 == q, v, acc)
        squares[:, t * LANE : (t + 1) * LANE] = acc * acc * (1.0 / 64.0)

    corners = 1.0 - offs[...].astype(F32) * (1.0 / 16.0)

    def sign(d, axis):
        return corners[axis : axis + 1, d : d + 1]

    own_dom = lax.broadcasted_iota(jnp.int32, (1, 8), 1) == dom
    sign_y = jnp.sum(jnp.where(own_dom, corners[1:2], 0.0), axis=1, keepdims=True)
    odd_row = lax.broadcasted_iota(jnp.int32, (GRID, 32), 0) >= 32
    parts = dot(jnp.where(odd_row, sign_y, 1.0) * by[...], squares[...])
    for x in range(4):
        p_send[x] = parts[16 * x : 16 * x + 16]

    def x_copy(x, slot):
        return pltpu.make_async_remote_copy(
            src_ref=p_send.at[x], dst_ref=x_recv.at[slot], send_sem=xs.at[x],
            recv_sem=xr.at[slot], device_id=at_x(x), device_id_type=MESH,
        )

    for o in (2, 1, 3):
        x_copy(turn(xi + o, 4), xi).start()
    x_recv[xi] = p_send[xi]
    halo2 = pltpu.make_async_remote_copy(
        src_ref=buf_a.at[2:10, 8:48, :], dst_ref=h2_recv, send_sem=h2_sems.at[0],
        recv_sem=h2_sems.at[1], device_id=at_x(partner), device_id_type=MESH,
    )
    halo2.start()
    for o in (1, 3, 2):
        x_copy(turn(xi + o, 4), turn(xi - o + 4, 4)).wait_recv()
    for h in range(2):
        both = x_recv[h] + x_recv[h + 2]
        for t in range(4):
            y_send[pl.ds(h * 4 + t, 16, stride=8), :] = both[:, t * LANE : (t + 1) * LANE]

    def rows(index, size):
        return pl.ds(pl.multiple_of(index * size, 8), size)

    def y_copy(c, slot):
        return pltpu.make_async_remote_copy(
            src_ref=y_send.at[rows(c, 8)], dst_ref=y_recv.at[rows(slot, 8)], send_sem=ys,
            recv_sem=yr, device_id=at_y(c), device_id_type=MESH,
        )

    def whole(ref, send_sem, recv_sem):
        return pltpu.make_async_remote_copy(
            src_ref=ref, dst_ref=ref, send_sem=send_sem, recv_sem=recv_sem,
            device_id=at_x(partner), device_id_type=MESH,
        )

    y_whole = whole(y_recv.at[0:120], ys, yr)
    f_whole = whole(f_recv.at[0 : 48 * USED], fs, fr)

    pl.semaphore_wait(ready3, 4)
    for o in FAR:
        y_copy(turn(yc + o, 16), yc).start()
    y_recv[rows(yc, 8), :] = y_send[rows(yc, 8), :]
    y_whole.wait_recv()

    d_all = y_recv[0:64, :] + y_recv[64:128, :]
    lane64 = lanes((64, LANE))
    masked = jnp.concatenate([jnp.where(lane64 // 32 == q, d_all, 0.0) for q in range(4)], 0)
    v_all = dot(masked, cz[...])
    lane8 = lanes((8, LANE))
    signs = []
    for d in range(8):
        sign_z = jnp.where(lane8 % 64 >= 32, sign(d, 2), 1.0)
        signs.append(sign_z * jnp.where(lane8 >= 64, sign(d, 0), 1.0))
    v_all = v_all * jnp.concatenate(signs * 4, 0)
    o_all = dot(cx[...], v_all)
    lane_r = lanes((32, LANE))
    left = lane_r < 64
    r2 = jnp.where(left, o_all[0:32], o_all[32:64])
    z_send[...] = r2

    sums = (zi >= SUMS[0]) | (zi == SUMS[3])
    tile_of = jnp.where(zi == SUMS[3], 3, zi - SUMS[0])

    def z_copy(t, slot):
        return pltpu.make_async_remote_copy(
            src_ref=z_send.at[8 * t : 8 * t + 8], dst_ref=z_recv.at[rows(slot, 8)], send_sem=zs,
            recv_sem=zr, device_id=at_z(SUMS[t]), device_id_type=MESH,
        )

    for t in range(4):

        @pl.when(zi != SUMS[t])
        def _():
            z_copy(t, zi).start()

    @pl.when(sums)
    def _():
        z_recv[rows(zi, 8), :] = z_send[rows(tile_of, 8), :]
        whole(z_recv.at[0:120], zs, zr).wait_recv()
        total = z_recv[0:8]
        for k in range(1, 16):
            total = total + z_recv[8 * k : 8 * k + 8]
        z_all[rows(tile_of, 8), :] = total
        for z in SUM_TO:

            @pl.when(zi != z)
            def _():
                pltpu.make_async_remote_copy(
                    src_ref=z_all.at[rows(tile_of, 8)], dst_ref=z_all.at[rows(tile_of, 8)],
                    send_sem=as_, recv_sem=ar, device_id=at_z(z), device_id_type=MESH,
                ).start()

        whole(z_all.at[0:24], as_, ar).wait_recv()

    @pl.when(jnp.logical_not(sums))
    def _():
        whole(z_all.at[0:32], as_, ar).wait_recv()

    r2 = z_all[...]
    lam = lam2[...] + lam_y[pl.ds(xi * 16 + yc, 1), :]
    factor = jnp.where(lam == 0.0, 0.0, 4.0 * math.pi / jnp.where(lam == 0.0, 1.0, lam))
    phi2 = r2 * factor
    top = jnp.where(left, r2, roll(phi2, 64))
    bottom = jnp.where(left, roll(r2, 64), phi2)
    t_all = dot(xall[...], jnp.concatenate([top, bottom], 0))
    t0, t1, t2 = t_all[0:40], t_all[40:80], t_all[80:120]
    left40 = lanes((40, LANE)) < 64
    of_rho = jnp.concatenate([jnp.where(left40, t0, roll(t1, 64)), t2], 1)
    of_phi = jnp.concatenate([jnp.where(left40, roll(t0, 64), t1), roll(t2, 64)], 1)
    planes = dot(jnp.concatenate([of_rho, of_phi], 0), zt[...])
    for d in range(8):
        both = planes[:, 0:LANE] + sign(d, 2) * planes[:, LANE : 2 * LANE]
        for f in range(2):
            rows20 = both[40 * f : 40 * f + 20] + sign(d, 0) * both[40 * f + 20 : 40 * f + 40]
            for h in range(2):
                at = (2 * d + h) * PART + 10 * f
                c_send[at : at + 10, :] = rows20[10 * h : 10 * h + 10]

    def used(index):
        return pl.ds(pl.multiple_of(index * PART, 8), USED)

    def c_copy(c, slot, h):
        return pltpu.make_async_remote_copy(
            src_ref=c_send.at[used(2 * (c - jnp.where(c >= 8, 8, 0)) + h)],
            dst_ref=c_recv.at[used(2 * slot + h)], send_sem=cs,
            recv_sem=cr.at[slot], device_id=at_y(c), device_id_type=MESH,
        )

    for o in NEAR:
        for h in range(2):
            c_copy(turn(yc + o, 16), yc, h).start()
    c_recv[rows(yc, 2 * PART), :] = c_send[rows(dom, 2 * PART), :]

    def f_copy(x, h, c, from_x):
        return pltpu.make_async_remote_copy(
            src_ref=c_recv.at[used(2 * c + h)],
            dst_ref=f_recv.at[used(from_x * 16 + c)],
            send_sem=fs, recv_sem=fr,
            device_id=at_x(x), device_id_type=MESH,
        )

    def forward(c):
        for o in (2, 1, 3):
            f_copy(turn(xi + o, 4), s if o == 2 else 1 - s, c, xi).start()
        f_recv[rows(xi * 16 + c, PART), :] = c_recv[rows(2 * c + s, PART), :]

    forward(yc)

    y_whole.wait_send()

    @pl.when(sums)
    def _():
        whole(z_send.at[0:24], zs, zr).wait_send()
        whole(z_recv.at[0:120], as_, ar).wait_send()

    @pl.when(jnp.logical_not(sums))
    def _():
        whole(z_send.at[0:32], zs, zr).wait_send()

    for o in range(1, 4):
        x_copy(turn(xi + o, 4), xi).wait_send()

    for o in NEAR:
        c = turn(yc - o + 16, 16)
        whole(c_recv.at[0 : 2 * USED], cs, cr.at[c]).wait_recv()
        forward(c)

    halo2.wait()
    lane40 = lanes((SIDE, LANE))
    for r in range(ROWS):
        own = jnp.where(lane40 < 2 * GAP, buf_a[r, 8:48, :], 0.0)
        if r < HALO:
            inside = (lane40 >= 2 * GAP) & (lane40 < 2 * GAP + SIDE)
            own = jnp.where(inside, roll(h2_recv[HALO - 1 - r], GAP), own)
        field[r] = own

    f_whole.wait_recv()

    odd_col = lanes((SIDE, GRID)) >= 32
    to_y = jnp.where(odd_col, sign_y, 1.0) * yt[...]
    for r in range(ROWS):
        rho = dot(to_y, f_recv[pl.ds(r, GRID, stride=PART), :])
        phi = dot(to_y, f_recv[pl.ds(ROWS + r, GRID, stride=PART), :])
        coef_out[r] = coef[r] + (phi + EXCHANGE * cbrt(rho)) * (2.0 / HALF_WIDTH)
    whole(c_recv.at[0 : 30 * USED], cs, cs).wait_send()
    f_whole.wait_send()


def last_kernel(field, coef, out, buf_a, buf_b, lines):
    band = lax.axis_index("band")
    s = lax.rem(band, 2)
    clear_edges(buf_a)
    clear_edges(buf_b)
    for r in range(ROWS):
        buf_a[r, 8:48, :] = field[r]
    chebyshev(buf_a, buf_b, coef)
    for slot in range(20):
        g, r = divmod(slot, ROWS)
        row = slot + s * (19 - 2 * slot)
        lines[pl.ds(row, SIDE, stride=24), :] = roll(buf_a[r, 8:48, :], -GAP * g)
    lane = lanes((24, LANE))
    for block in range(13):
        acc = jnp.zeros((24, LANE), F32)
        for y in range(SIDE):
            start = SIDE * y - LANE * block
            if start + SIDE > 0 and start < LANE:
                v = roll(lines[y * 24 : y * 24 + 24, :], start)
                inside = (lane >= start) & (lane < start + SIDE)
                acc = jnp.where(inside, v, acc)
        width = min(LANE, 1600 - LANE * block)
        for x in range(20):
            out[x, :, block * LANE : block * LANE + width] = acc[x : x + 1, 0:width]


def local(psi_in, v_in, offsets):
    consts = tables()
    vmem = pl.BlockSpec(memory_space=pltpu.VMEM)
    dma = pltpu.SemaphoreType.DMA
    tile = jax.ShapeDtypeStruct((ROWS, SIDE, LANE), F32)

    def scratch(*shape):
        return pltpu.VMEM(shape, F32)

    operands = (
        offsets.T, jnp.swapaxes(psi_in[0], 0, 1), v_in[0], *[jnp.asarray(a) for a in consts]
    )
    field, coef = pl.pallas_call(
        main_kernel,
        out_shape=(tile, tile),
        in_specs=[pl.BlockSpec(memory_space=pltpu.HBM)] * (3 + TABLES),
        out_specs=(vmem, vmem),
        scratch_shapes=[
            *[scratch(*a.shape) for a in consts], pltpu.VMEM((3, 8), jnp.int32),
            scratch(20, 1, 1600), scratch(40, 1600), dma((3 + TABLES,)),
            scratch(24, 1664), scratch(40, 1664), scratch(40 * 32, LANE), scratch(40 * 40, LANE),
            scratch(8, 1664), scratch(HALO, 1, 1600), scratch(ROWS, 56, LANE), scratch(ROWS, 56, LANE),
            scratch(ROWS, SIDE, LANE), scratch(32, 512),
            scratch(4, 16, 512), scratch(4, 16, 512), scratch(128, LANE), scratch(128, LANE),
            scratch(32, LANE), scratch(128, LANE), scratch(32, LANE),
            scratch(16 * PART, LANE), scratch(32 * PART, LANE), scratch(64 * PART, LANE),
            scratch(HALO, SIDE, LANE),
            pltpu.SemaphoreType.REGULAR, pltpu.SemaphoreType.REGULAR,
            dma((2,)), dma((2,)), dma((4,)), dma((4,)), dma, dma, dma, dma, dma, dma,
            dma, dma((16,)), dma, dma,
        ],
        compiler_params=pltpu.CompilerParams(collective_id=0, has_side_effects=True, vmem_limit_bytes=24 << 20
        ),
        name="step",
    )(*[pltpu.with_memory_space_constraint(a, pltpu.HBM) for a in operands])
    out = pl.pallas_call(
        last_kernel,
        out_shape=jax.ShapeDtypeStruct((20, 1, 1600), F32),
        in_specs=[vmem, vmem],
        out_specs=vmem,
        scratch_shapes=[
            scratch(ROWS, 56, LANE), scratch(ROWS, 56, LANE), scratch(40 * 24, LANE),
        ],
        compiler_params=pltpu.CompilerParams(vmem_limit_bytes=8 << 20),
        name="last",
    )(field, coef)
    return jnp.swapaxes(out, 0, 1)[None]


def solution(mesh):
    return jax.shard_map(
        local,
        mesh=mesh,
        in_specs=(P("dom", "band", None, None), P("dom", None, None), P()),
        out_specs=P("dom", "band", None, None),
        check_vma=False,
    )
```
